128 devices in a mesh: sector: 16 (over x, z_lo, core), slab: 8 (over y, z_hi).
Axes of the slice: x: 4, y: 4, z: 4 (z_hi: 2, z_lo: 2; z = z_hi * 2 + z_lo), core: 2. Of those that a mesh axis runs over, the one named last changes fastest.
Arguments:
- right_basis: float32 [64, 128, 96, 256], P(None, 'sector', 'slab')
- left_basis: float32 [64, 128, 96, 256], P(None, 'sector', 'slab')
- speed_squared: float32 [128, 96, 256], P('sector', 'slab'), may hold values from 0.5 to 8
- rayleigh: float32 [64, 64], replicated
- schur_order: int32 [64], replicated, may hold values from 0 to 63, each once
- kept_index: int32 [32], replicated, may hold values from 0 to 63, as said below
- rim_map: int32 [256], replicated, may hold values from 0 to 255, each once
Outputs:
- new_right: float32 [32, 128, 96, 256], P(None, 'sector', 'slab')
- new_left: float32 [32, 128, 96, 256], P(None, 'sector', 'slab')
- right_image: float32 [32, 128, 96, 256], P(None, 'sector', 'slab')
- left_image: float32 [32, 128, 96, 256], P(None, 'sector', 'slab')
- restarted: float32 [32, 32], replicated
The draws below stay inside these ranges and needn't reach their ends.
Inputs may be any that keep to these rules, and one draw needn't show every extreme that they name: `kept_index`: 32 distinct basis indices, 0 and 63 among them. `schur_order`: each basis index once. `rim_map`: each radial cell once.
All inputs are finite; a program needn't handle non-finite values.
Results may differ from the reference program's by a relative error of at most 0.0003.
Values sent between devices are 32-bit elements; how exact they have to be, the bound alone decides.
A program may use at most 256 MiB of HBM per device.

```python
import math
import jax
import jax.numpy as jnp
from jax import lax

K = 64
KEEP = 32
CT = 8
CR = 256
NT = 128
NA = 96


def paired_bases(key):
    subkeys = [jax.random.fold_in(key, 7001 + number) for number in range(8)]
    fresh = jax.random.normal(subkeys[0], (K + 1, NT, NA, CR), jnp.float32)
    mixed = fresh[:-1] + 0.6 * fresh[1:]
    theta_ramp = 1.0 + 2.0 * jnp.arange(NT, dtype=jnp.float32) / max(NT - 1, 1)
    axial_ramp = 1.0 + 2.0 * jnp.arange(NA, dtype=jnp.float32) / max(NA - 1, 1)
    rough = jnp.exp(jax.random.uniform(subkeys[2], (NT, NA, CR), jnp.float32, 0.0, math.log(10.0)))
    scale = 0.25 * theta_ramp[:, None, None] * axial_ramp[None, :, None] * rough
    right = scale[None] * mixed
    weight = jnp.exp(jax.random.uniform(subkeys[3], (NT, NA, CR), jnp.float32, math.log(0.5), math.log(2.0)))
    own_size = jnp.exp(jax.random.uniform(subkeys[5], (K,), jnp.float32, 0.0, math.log(2.0)))
    own_sign = jax.random.rademacher(subkeys[6], (K,), jnp.float32)
    own_coeff = (own_size * own_sign)[:, None, None, None]
    next_coeff = jax.random.uniform(subkeys[7], (K,), jnp.float32, -0.5, 0.5)[:, None, None, None]
    blended = own_coeff * right + next_coeff * jnp.roll(right, 1, axis=0)
    left = weight[None] * blended + 0.7 * scale[None] * jax.random.normal(subkeys[4], (K, NT, NA, CR), jnp.float32)
    return (right, left)


def draw_right_basis(key, part):
    return paired_bases(key)[0]


def draw_left_basis(key, part):
    return paired_bases(key)[1]


def draw_rayleigh(key, part):
    subkeys = [jax.random.fold_in(key, 8101 + number) for number in range(3)]
    magnitude = jnp.exp(jax.random.uniform(subkeys[0], (K,), jnp.float32, 0.0, math.log(4.0)))
    signs = jax.random.rademacher(subkeys[1], (K,), jnp.float32)
    spread_vectors = jax.random.normal(subkeys[2], (K, K), jnp.float32) * (0.5 / math.sqrt(K))
    return jnp.diag(magnitude * signs) + spread_vectors


def draw_kept_index(key, part):
    subkeys = [jax.random.fold_in(key, 9201 + number) for number in range(2)]
    middle = (jax.random.permutation(subkeys[0], K - 2) + 1).astype(jnp.int32)
    chosen = jnp.concatenate([jnp.array([0, K - 1], jnp.int32), middle[:KEEP - 2]])
    return jax.random.permutation(subkeys[1], chosen).astype(jnp.int32)


def block_levels(key, extent, split, low, top_value):
    def one(position, blocks):
        steps = jax.random.uniform(jax.random.fold_in(jax.random.fold_in(key, 6), position), (blocks,), jnp.float32, low / len(split), top_value / len(split))
        return jnp.repeat(jnp.exp(steps), extent[position] // blocks).reshape((-1,) + (1,) * (len(extent) - position - 1))

    level = one(*split[0])
    for cut in split[1:]:
        level = level * one(*cut)
    return level


def setup_inputs(seed: int = 0) -> dict:
    key_list = jax.random.split(jax.random.key(seed), 8)
    return {
        "right_basis": draw_right_basis(jax.random.fold_in(key_list[7], 71), 0),
        "left_basis": draw_left_basis(jax.random.fold_in(key_list[7], 71), 0),
        "speed_squared": jnp.clip(jnp.exp(math.log(8.0) - 2.7725887 * jax.random.uniform(key_list[2], (NT, NA, CR), jnp.float32) ** block_levels(key_list[2], (NT, NA, CR), ((0, 16), (1, 8)), -0.2, 0.2)), 0.5, 8.0),
        "rayleigh": draw_rayleigh(jax.random.fold_in(key_list[7], 71), 0),
        "schur_order": jax.random.permutation(key_list[4], K).astype(jnp.int32),
        "kept_index": draw_kept_index(jax.random.fold_in(key_list[7], 71), 0),
        "rim_map": jax.random.permutation(key_list[6], CR).astype(jnp.int32),
    }


def exact_dot(left_operator, right_operator):
    return jnp.dot(left_operator, right_operator, precision=lax.Precision.HIGHEST)

def lower_inverse(lower_factor):
    identity = jnp.eye(lower_factor.shape[0], dtype=lower_factor.dtype)
    return lax.linalg.triangular_solve(lower_factor, identity, left_side=True, lower=True)

def solve_inverse(cross_matrix):
    normal_matrix = exact_dot(cross_matrix.T, cross_matrix)
    scaling_factor = jnp.linalg.cholesky(normal_matrix)
    middle = lax.linalg.triangular_solve(scaling_factor, cross_matrix.T, left_side=True, lower=True)
    return lax.linalg.triangular_solve(scaling_factor, middle, left_side=True, lower=True, transpose_a=True)

def orthonormal(matrix):

    def column_step(column_index, partial_basis):
        column_index = jnp.asarray(column_index).astype(jnp.int32)
        column = lax.dynamic_slice_in_dim(matrix, column_index, 1, 1)
        column = column - exact_dot(partial_basis, exact_dot(partial_basis.T, column))
        column = column - exact_dot(partial_basis, exact_dot(partial_basis.T, column))
        column = column / jnp.sqrt(jnp.sum(column * column))
        return lax.dynamic_update_slice_in_dim(partial_basis, column, column_index, 1)
    return lax.fori_loop(0, matrix.shape[1], column_step, jnp.zeros_like(matrix))

def select_matrix(chosen, total):
    return (jnp.arange(total)[:, None] == chosen[None, :]).astype(jnp.float32)

def small_step(lower_factor, lower_inverse_mat, cross_inverse, rayleigh, schur_order, kept_index):
    total = rayleigh.shape[0]
    turned = exact_dot(exact_dot(lower_factor.T, rayleigh), lower_inverse_mat.T)
    select_order = select_matrix(schur_order, total)
    permuted = exact_dot(exact_dot(select_order.T, turned), select_order)
    orthogonal = orthonormal(permuted)
    kept_basis = exact_dot(orthogonal, select_matrix(kept_index, total))
    restarted = exact_dot(exact_dot(kept_basis.T, permuted), kept_basis)
    return (restarted, exact_dot(kept_basis.T, lower_inverse_mat), exact_dot(kept_basis.T, cross_inverse))

def laplace(vector, rim_map, inverse_map):
    theta_index = jnp.arange(NT)
    forward = jnp.roll(vector, -1, axis=0)
    forward = jnp.where((theta_index % CT == CT - 1)[:, None, None], forward[:, :, rim_map], forward)
    behind = jnp.roll(vector, 1, axis=0)
    behind = jnp.where((theta_index % CT == 0)[:, None, None], behind[:, :, inverse_map], behind)
    padded = jnp.pad(vector, ((0, 0), (1, 1), (1, 1)))
    final_result = 6.0 * vector - forward - behind
    final_result = final_result - padded[:, 2:, 1:-1] - padded[:, :-2, 1:-1]
    return final_result - padded[:, 1:-1, 2:] - padded[:, 1:-1, :-2]

def reference(right_basis, left_basis, speed_squared, rayleigh, schur_order, kept_index, rim_map):
    right_rows = right_basis.reshape(K, -1)
    left_rows = left_basis.reshape(K, -1)
    row_total = right_rows.shape[1]
    right_gram = exact_dot(right_rows, right_rows.T) / row_total
    lower_factor = jnp.linalg.cholesky(right_gram)
    lower_inverse_mat = lower_inverse(lower_factor)
    normalized = exact_dot(lower_inverse_mat, right_rows)
    cross_matrix = exact_dot(left_rows, normalized.T) / row_total
    cross_inverse = solve_inverse(cross_matrix)
    restarted, rotate_right, rotate_left = small_step(lower_factor, lower_inverse_mat, cross_inverse, rayleigh, schur_order, kept_index)
    new_right = exact_dot(rotate_right, right_rows)
    new_left = exact_dot(rotate_left, left_rows)
    flat_speed = speed_squared.reshape(1, -1)
    inverse_map = jnp.zeros((CR,), jnp.int32).at[rim_map].set(jnp.arange(CR, dtype=jnp.int32))
    stacked = jnp.concatenate([new_right, flat_speed * new_left], axis=0).reshape((2 * KEEP,) + speed_squared.shape)
    applied = lax.map(lambda single_field: laplace(single_field, rim_map, inverse_map), stacked).reshape(2 * KEEP, -1)
    right_image = flat_speed * applied[:KEEP] - new_right
    left_image = applied[KEEP:] - new_left
    out_shape = (KEEP,) + speed_squared.shape
    return (new_right.reshape(out_shape), new_left.reshape(out_shape), right_image.reshape(out_shape), left_image.reshape(out_shape), restarted)
```

```python
import jax
import jax.numpy as jnp
from jax import lax
from jax.experimental import pallas as pl
from jax.experimental.pallas import tpu as pltpu
from jax.sharding import PartitionSpec as P

MESH = pl.DeviceIdType.MESH
NN = (((1,), (0,)), ((), ()))
NT = (((1,), (1,)), ((), ()))
TN = (((0,), (0,)), ((), ()))
F32 = jnp.float32
BF16 = jnp.bfloat16
K, KEEP, CT, CA, CR = 64, 32, 8, 12, 256
CELLS = 3145728


def mm(a, b, dims=NN):
    return lax.dot_general(a, b, dims, precision=lax.Precision.HIGHEST, preferred_element_type=F32)


def mm16(a, b, dims=NN):
    return lax.dot_general(a, b, dims, preferred_element_type=F32)


def iota(shape, dim):
    return lax.broadcasted_iota(jnp.int32, shape, dim)


def split(x):
    high = x.astype(BF16)
    return high, (x - high.astype(F32)).astype(BF16)


def stacked(right, left):
    return jnp.concatenate(split(right) + split(left), axis=0)


def halves(pair):
    return jnp.concatenate(pair, axis=1)


def gram_kernel(right_ref, left_ref, speed_ref, rim_ref, part_ref, cells_ref, ang_ref, ax_ref, buf_ref, sem):
    refs = (right_ref, left_ref)

    @pl.loop(0, CA)
    def _(a):
        for n in range(2):
            for t in range(CT):
                for j in range(2):
                    pltpu.make_async_copy(refs[n].at[:, a, j, t, :], buf_ref.at[a, n, t, j], sem.at[a]).start()

    part_ref[...] = jnp.zeros_like(part_ref)
    hot = (iota((CR, CR), 0) == rim_ref[...]).astype(BF16)

    def scaled(a, t):
        fields = []
        for j in range(2):
            fields.append(speed_ref[a, j, t:t + 1, :] * buf_ref[a, 1, t, j])
        return split(halves(fields))

    def axial(side, a):
        for t in range(CT):
            plain = cells_ref[a, 0:128, t * CR:(t + 1) * CR]
            ax_ref[side, t] = jnp.concatenate((plain,) + scaled(a, t), axis=0)

    @pl.loop(0, CA)
    def _(a):
        pltpu.make_async_copy(buf_ref.at[a], buf_ref.at[a], sem.at[a]).wait()
        columns = []
        for t in range(CT):
            for j in range(2):
                columns.append(stacked(buf_ref[a, 0, t, j], buf_ref[a, 1, t, j]))
        x = halves(columns)
        cells_ref[a] = x
        part_ref[...] += mm16(x[:128], x, NT)
        for side, t in ((0, 0), (1, CT - 1)):
            edge = jnp.concatenate((x[:128, t * CR:(t + 1) * CR],) + scaled(a, t), axis=0)
            ang_ref[side, a] = mm16(edge, hot, NT if side else NN).astype(BF16)

        @pl.when(a == 0)
        def _():
            axial(0, a)

        @pl.when(a == CA - 1)
        def _():
            axial(1, a)


def gram(right, left, speed, rim):
    vmem = pl.BlockSpec(memory_space=pltpu.VMEM)
    main = pl.BlockSpec(memory_space=pltpu.HBM)
    return pl.pallas_call(
        gram_kernel,
        in_specs=[main, main, vmem, vmem],
        out_specs=[vmem] * 4,
        out_shape=[
            jax.ShapeDtypeStruct((128, 256), F32),
            pltpu.VMEM((CA, 256, CT * CR), BF16),
            jax.ShapeDtypeStruct((2, CA, 256, CR), BF16),
            jax.ShapeDtypeStruct((2, CT, 256, CR), BF16),
        ],
        scratch_shapes=[pltpu.VMEM((CA, 2, CT, 2, 64, 128), F32), pltpu.SemaphoreType.DMA((CA,))],
        compiler_params=pltpu.CompilerParams(vmem_limit_bytes=20 << 20),
        name="gram",
    )(pltpu.with_memory_space_constraint(right, pltpu.HBM), pltpu.with_memory_space_constraint(left, pltpu.HBM), speed, rim)


def place(sector, slab):
    return sector // 4, slab // 2, (slab % 2) * 2 + (sector // 2) % 2, sector % 2


def device(x, y, z, core):
    return (x * 4 + (z % 2) * 2 + core, y * 2 + z // 2)


def combined(part):
    top = part[:64] + part[64:]
    gram, cross = top[:, :128], top[:, 128:]
    gram, cross = gram + pltpu.roll(gram, 64, 1), cross + pltpu.roll(cross, 64, 1)
    return jnp.where(iota((64, 128), 1) < 64, gram, cross)


def reduce_kernel(raw_ref, out_ref, part_ref, got_ref, send_sem, recv_sem):
    part_ref[...] = combined(raw_ref[...])
    x, y, z, core = place(lax.axis_index("sector"), lax.axis_index("slab"))
    other = device(x, y, z, 1 - core)
    groups = (
        (x, [device(lax.rem(x + o, 4), y, z, core) for o in (1, 2, 3)]),
        (y, [device(x, lax.rem(y + o, 4), z, core) for o in (1, 2, 3)]),
        (z, [device(x, y, lax.rem(z + o, 4), core) for o in (1, 2, 3)]),
    )
    barrier = pltpu.get_barrier_semaphore()
    for peer in [other] + [p for _, peers in groups for p in peers]:
        pl.semaphore_signal(barrier, inc=1, device_id=peer, device_id_type=MESH)
    pl.semaphore_wait(barrier, 10)

    def send(src, dst, n, peer):
        copy = pltpu.make_async_remote_copy(
            src_ref=src, dst_ref=dst, send_sem=send_sem.at[n], recv_sem=recv_sem.at[n],
            device_id=peer, device_id_type=MESH)
        copy.start()
        return copy

    def half(h):
        return pl.ds(pl.multiple_of(h * 32, 32), 32)

    copies = [send(part_ref.at[half(1 - core)], got_ref.at[0, 0], 0, other)]
    copies[0].wait_recv()
    mine, theirs = part_ref[half(core), :], got_ref[0, 0]
    total = mine + theirs
    n = 1
    for stage, (me, peers) in enumerate(groups):
        got_ref[stage + 1, me] = total
        sent = []
        for peer in peers:
            sent.append(send(got_ref.at[stage + 1, me], got_ref.at[stage + 1, me], n, peer))
            n += 1
        for copy in sent:
            copy.wait_recv()
        copies += sent
        total = (got_ref[stage + 1, 0] + got_ref[stage + 1, 1]) + (got_ref[stage + 1, 2] + got_ref[stage + 1, 3])
    out_ref[half(core), :] = total
    copies.append(send(out_ref.at[half(core)], out_ref.at[half(core)], n, other))
    copies[-1].wait_recv()
    for copy in copies:
        copy.wait_send()


def reduced(part):
    vmem = pl.BlockSpec(memory_space=pltpu.VMEM)
    return pl.pallas_call(
        reduce_kernel,
        in_specs=[vmem],
        out_specs=vmem,
        out_shape=jax.ShapeDtypeStruct((64, 128), F32),
        scratch_shapes=[pltpu.VMEM((64, 128), F32), pltpu.VMEM((4, 4, 32, 128), F32), pltpu.SemaphoreType.DMA((11,)), pltpu.SemaphoreType.DMA((11,))],
        compiler_params=pltpu.CompilerParams(collective_id=0, has_side_effects=True, vmem_limit_bytes=4 << 20),
        name="reduced",
    )(part)


def pivot(a, k, rows):
    scaled = a[k:k + 1, :] * (1.0 / a[k:k + 1, k:k + 1])
    return a - jnp.where(rows > k, a[:, k:k + 1], 0.0) * scaled


def unit_rows(a, eye):
    return a * lax.rsqrt(jnp.sum(a[:, :64] * eye, axis=1, keepdims=True))


def small_step(gc, rayleigh, order, kept):
    rows = iota((64, 1), 0)
    r64, c64 = iota((64, 64), 0), iota((64, 64), 1)
    eye = (r64 == c64).astype(F32)
    order_col = jnp.sum(jnp.where(r64 == c64, order, 0).astype(F32), axis=1, keepdims=True).astype(jnp.int32)
    kept_col = jnp.sum(jnp.where(iota((32, 32), 0) == iota((32, 32), 1), kept, 0).astype(F32), axis=1, keepdims=True).astype(jnp.int32)
    select_order = (order_col == c64).astype(F32)
    select_kept = (kept_col == iota((32, 64), 1)).astype(F32)
    cross_t = gc[:, 64:]
    a1 = jnp.concatenate([gc[:, :64], eye], axis=1)
    a2 = jnp.concatenate([mm(cross_t, cross_t, NT), eye], axis=1)
    for k in range(64):
        a1 = pivot(a1, k, rows)
        a2 = pivot(a2, k, rows)
    a1, a2 = unit_rows(a1, eye), unit_rows(a2, eye)
    lower_t, lower_inv, cross_low = a1[:, :64], a1[:, 64:], a2[:, 64:]
    side = mm(lower_inv, rayleigh, NT)
    ordered = mm(select_order, jnp.concatenate([lower_t, side], axis=1))
    permuted_t = mm(ordered[:, 64:], ordered[:, :64], NT)
    a3 = jnp.concatenate([mm(permuted_t, permuted_t, NT), permuted_t], axis=1)
    cross_inv = mm(cross_low, mm(cross_low, cross_t), TN)
    cross_inv = cross_inv + mm(cross_inv, eye - mm(cross_t, cross_inv, TN))
    tail = jnp.concatenate([lower_inv, mm(lower_t, cross_inv)], axis=1)
    for k in range(64):
        a3 = pivot(a3, k, rows)
    basis_t = unit_rows(a3, eye)[:, 64:]
    weight = jnp.where(r64 > c64, 1.0, jnp.where(r64 == c64, 0.5, 0.0))
    for _ in range(2):
        basis_t = basis_t - mm((mm(basis_t, basis_t, NT) - eye) * weight, basis_t)
    kept_t = mm(select_kept, basis_t)
    restarted = mm(mm(kept_t, permuted_t, NT), kept_t, NT)
    return mm(kept_t, tail), restarted


def rotation_blocks(rotation):
    high, low = split(rotation)
    zero = jnp.zeros((KEEP, 128), BF16)

    def both(part):
        right, left = part[:, :64], part[:, 64:]
        return [
            jnp.concatenate([right, right, zero], axis=1),
            jnp.concatenate([zero, left, left], axis=1),
        ]

    return jnp.concatenate(both(high) + both(low), axis=0)


def small_kernel(gc_ref, rayleigh_ref, order_ref, kept_ref, rotate_ref, restarted_ref):
    rotation, restarted = small_step(gc_ref[...] * (1.0 / CELLS), rayleigh_ref[...], order_ref[...], kept_ref[...])
    rotate_ref[...] = rotation_blocks(rotation)
    restarted_ref[...] = restarted


def small(gc, rayleigh, order, kept):
    vmem = pl.BlockSpec(memory_space=pltpu.VMEM)
    return pl.pallas_call(
        small_kernel,
        in_specs=[vmem] * 4,
        out_specs=[vmem] * 2,
        out_shape=[jax.ShapeDtypeStruct((128, 256), BF16), jax.ShapeDtypeStruct((KEEP, KEEP), F32)],
        compiler_params=pltpu.CompilerParams(vmem_limit_bytes=6 << 20),
        name="small",
    )(gc, rayleigh, order, kept)


def rotated(rotate, block):
    both = mm16(rotate, block)
    return both[:64] + both[64:]


def halo_kernel(rotate_ref, ang_ref, ax_ref, ang_out, ax_out, ang_buf, ax_buf, send_sem, recv_sem):
    sector, slab = lax.axis_index("sector"), lax.axis_index("slab")
    targets = (
        (lax.rem(sector + 15, 16), slab),
        (lax.rem(sector + 1, 16), slab),
        (sector, lax.rem(slab + 7, 8)),
        (sector, lax.rem(slab + 1, 8)),
    )
    barrier = pltpu.get_barrier_semaphore()
    for target in targets:
        pl.semaphore_signal(barrier, inc=1, device_id=target, device_id_type=MESH)
    rotate = rotate_ref[...]
    copies = []
    for n, target in enumerate(targets):
        buf, out = ((ang_buf, ang_out), (ax_buf, ax_out))[n // 2]
        side = n % 2
        copies.append(pltpu.make_async_remote_copy(
            src_ref=buf.at[side], dst_ref=out.at[1 - side], send_sem=send_sem.at[n], recv_sem=recv_sem.at[n],
            device_id=target, device_id_type=MESH))

    def fill(n):
        buf, ref = ((ang_buf, ang_ref), (ax_buf, ax_ref))[n // 2]
        side = n % 2

        @pl.loop(0, buf.shape[1])
        def _(i):
            buf[side, i] = rotated(rotate, ref[side, i])

    fill(2)
    pl.semaphore_wait(barrier, 4)

    @pl.when(slab > 0)
    def _():
        copies[2].start()

    fill(3)

    @pl.when(slab < 7)
    def _():
        copies[3].start()

    fill(0)
    copies[0].start()
    fill(1)
    copies[1].start()
    copies[0].wait()
    copies[1].wait()

    @pl.when(slab > 0)
    def _():
        copies[2].wait_send()
        copies[3].wait_recv()

    @pl.when(slab < 7)
    def _():
        copies[3].wait_send()
        copies[2].wait_recv()


def halos(rotate, ang, ax):
    vmem = pl.BlockSpec(memory_space=pltpu.VMEM)
    anywhere = pl.BlockSpec(memory_space=pl.ANY)
    return pl.pallas_call(
        halo_kernel,
        in_specs=[vmem] * 3,
        out_specs=[anywhere] * 2,
        out_shape=[jax.ShapeDtypeStruct((2, CA, 64, CR), F32), jax.ShapeDtypeStruct((2, CT, 64, CR), F32)],
        scratch_shapes=[pltpu.VMEM((2, CA, 64, CR), F32), pltpu.VMEM((2, CT, 64, CR), F32),
                        pltpu.SemaphoreType.DMA((4,)), pltpu.SemaphoreType.DMA((4,))],
        compiler_params=pltpu.CompilerParams(collective_id=1, has_side_effects=True, vmem_limit_bytes=8 << 20),
        name="halos",
    )(rotate, ang, ax)


def image_kernel(rotate_ref, cells_ref, speed_ref, ang_ref, ax_ref, new_right_ref, new_left_ref, right_image_ref,
                 left_image_ref, field_ref, plain_ref, image_ref, sem):
    slab = lax.axis_index("slab")
    outs = (new_right_ref, new_left_ref, right_image_ref, left_image_ref)
    rotate = rotate_ref[...]
    zero = jnp.zeros((64, 128), F32)

    @pl.loop(0, CT)
    def _(t):
        for j in range(2):
            field_ref[0, t, j] = jnp.where(slab > 0, ax_ref[0, t, :, j * 128:(j + 1) * 128], zero)
            field_ref[CA + 1, t, j] = jnp.where(slab < 7, ax_ref[1, t, :, j * 128:(j + 1) * 128], zero)

    def send(n, src, a, t, j):
        pltpu.make_async_copy(src, outs[n].at[:, a, j, t, :], sem.at[n]).start()

    @pl.loop(0, CA + 1)
    def _(step):
        @pl.when(step < CA)
        def _():
            a = step
            for t in range(CT):
                value = rotated(rotate, cells_ref[a, :, t * CR:(t + 1) * CR])
                for j in range(2):
                    part = value[:, j * 128:(j + 1) * 128]
                    field_ref[a + 1, t, j, 0:KEEP] = part[:KEEP]
                    field_ref[a + 1, t, j, KEEP:] = part[KEEP:] * speed_ref[a, j, t:t + 1, :]
                    plain_ref[a, t, j] = part[KEEP:]
            for t in range(CT):
                for j in range(2):
                    send(0, field_ref.at[a + 1, t, j, 0:KEEP], a, t, j)
                    send(1, plain_ref.at[a, t, j], a, t, j)

        @pl.when(step > 0)
        def _():
            a = step - 1
            lanes = iota((64, 128), 1)
            for t in range(CT):
                mid = [field_ref[a + 1, t, j] for j in range(2)]
                up = [pltpu.roll(m, 1, 1) for m in mid]
                down = [pltpu.roll(m, 127, 1) for m in mid]
                behind = [jnp.where(lanes == 0, 0.0, up[0]), jnp.where(lanes == 0, up[0], up[1])]
                ahead = [jnp.where(lanes == 127, down[1], down[0]), jnp.where(lanes == 127, 0.0, down[1])]
                for j in range(2):
                    total = field_ref[a, t, j] + field_ref[a + 2, t, j]
                    total = total + (field_ref[a + 1, t - 1, j] if t > 0 else ang_ref[0, a, :, j * 128:(j + 1) * 128])
                    total = total + (field_ref[a + 1, t + 1, j] if t < CT - 1 else ang_ref[1, a, :, j * 128:(j + 1) * 128])
                    applied = 6.0 * mid[j] - total - behind[j] - ahead[j]
                    image_ref[a, t, j, 0:KEEP] = applied[:KEEP] * speed_ref[a, j, t:t + 1, :] - mid[j][:KEEP]
                    image_ref[a, t, j, KEEP:] = applied[KEEP:] - plain_ref[a, t, j]
            for t in range(CT):
                for j in range(2):
                    send(2, image_ref.at[a, t, j, 0:KEEP], a, t, j)
                    send(3, image_ref.at[a, t, j, KEEP:], a, t, j)

    for n in range(4):
        pltpu.make_async_copy(outs[n], outs[n], sem.at[n]).wait()


def images(rotate, cells, speed, ang, ax):
    vmem = pl.BlockSpec(memory_space=pltpu.VMEM)
    main = pl.BlockSpec(memory_space=pltpu.HBM)
    kept = jax.ShapeDtypeStruct((KEEP, CA, 2, CT, 128), F32)
    return pl.pallas_call(
        image_kernel,
        in_specs=[vmem] * 5,
        out_specs=[main] * 4,
        out_shape=[kept] * 4,
        scratch_shapes=[pltpu.VMEM((CA + 2, CT, 2, 64, 128), F32), pltpu.VMEM((CA, CT, 2, KEEP, 128), F32),
                        pltpu.VMEM((CA, CT, 2, 64, 128), F32), pltpu.SemaphoreType.DMA((4,))],
        compiler_params=pltpu.CompilerParams(vmem_limit_bytes=22 << 20),
        name="images",
    )(rotate, pltpu.with_memory_space_constraint(cells, pltpu.VMEM), speed, ang, ax)


def tiles(array):
    return array.reshape(array.shape[0], CT, CA, 2, 128).transpose(0, 2, 3, 1, 4)


def local(right_basis, left_basis, speed_squared, rayleigh, schur_order, kept_index, rim_map):
    right, left, speed = tiles(right_basis), tiles(left_basis), tiles(speed_squared[None])[0]
    part, cells, ang, ax = gram(right, left, speed, rim_map.reshape(1, CR))
    rotate, restarted = small(reduced(part), rayleigh, schur_order.reshape(1, K), kept_index.reshape(1, KEEP))
    ang_halo, ax_halo = halos(rotate, ang, ax)
    outs = images(rotate, cells, speed, ang_halo, ax_halo)
    shape = (KEEP, CT, CA, CR)
    return tuple(o.transpose(0, 3, 1, 2, 4).reshape(shape) for o in outs) + (restarted,)


def solution(mesh):
    fields = P(None, "sector", "slab", None)
    return jax.shard_map(
        local,
        mesh=mesh,
        in_specs=(fields, fields, P("sector", "slab", None), P(), P(), P(), P()),
        out_specs=(fields, fields, fields, fields, P()),
        check_vma=False,
    )
```

```python
import jax
import jax.numpy as jnp
from jax import lax
from jax.experimental import pallas as pl
from jax.experimental.pallas import tpu as pltpu
from jax.sharding import PartitionSpec as P

MESH = pl.DeviceIdType.MESH
NN = (((1,), (0,)), ((), ()))
NT = (((1,), (1,)), ((), ()))
TN = (((0,), (0,)), ((), ()))
F32 = jnp.float32
BF16 = jnp.bfloat16
K, KEEP, CT, CA, CR = 64, 32, 8, 12, 256
CELLS = 3145728
EARLY = 2
RAW = 4


def mm(a, b, dims=NN):
    return lax.dot_general(a, b, dims, precision=lax.Precision.HIGHEST, preferred_element_type=F32)


def mm16(a, b, dims=NN):
    return lax.dot_general(a, b, dims, preferred_element_type=F32)


def iota(shape, dim):
    return lax.broadcasted_iota(jnp.int32, shape, dim)


def split(x):
    high = x.astype(BF16)
    return high, (x - high.astype(F32)).astype(BF16)


def stacked(right, left):
    return jnp.concatenate(split(right) + split(left), axis=0)


def halves(pair):
    return jnp.concatenate(pair, axis=1)


def place(sector, slab):
    return sector // 4, slab // 2, (slab % 2) * 2 + (sector // 2) % 2, sector % 2


def device(x, y, z, core):
    return (x * 4 + (z % 2) * 2 + core, y * 2 + z // 2)


def combined(part):
    top = part[:64] + part[64:]
    gram, cross = top[:, :128], top[:, 128:]
    gram, cross = gram + pltpu.roll(gram, 64, 1), cross + pltpu.roll(cross, 64, 1)
    return jnp.where(iota((64, 128), 1) < 64, gram, cross)


def pivots(group, first):
    rows = iota((8, 128), 0)
    top = first // 8
    states = []
    for blocks in group:
        columns = [[jnp.broadcast_to(blocks[i][:, first + j:first + j + 1], (8, 128)) for i in range(top, 8)] for j in range(8)]
        corner = [[columns[j][0][i:i + 1, :] for j in range(8)] for i in range(8)]
        states.append((columns, corner, [blocks[top][i:i + 1, :] for i in range(8)], []))
    for j in range(8):
        for columns, corner, lead, scaled in states:
            inverse = 1.0 / corner[j][j]
            scaled.append(lead[j] * inverse)
            for m in range(j + 1, 8):
                factor = corner[m][j] * inverse
                for i in range(m, 8):
                    corner[i][m] = corner[i][m] - corner[i][j] * factor
                lead[m] = lead[m] - corner[m][j] * scaled[j]
                columns[m] = [c - d * factor for c, d in zip(columns[m], columns[j])]
    result = []
    for blocks, (columns, _, _, scaled) in zip(group, states):
        blocks = list(blocks)
        for i in range(top, 8):
            for j in range(8):
                column = columns[j][i - top]
                if i == top:
                    column = jnp.where(rows > j, column, 0.0)
                blocks[i] = blocks[i] - column * scaled[j]
        result.append(blocks)
    return result


def eliminate(arrays):
    rows, lanes = iota((8, 128), 0), iota((8, 128), 1)
    group = [[a[8 * i:8 * i + 8, :] for i in range(8)] for a in arrays]
    for first in range(0, 64, 8):
        group = pivots(group, first)
    result = []
    for blocks in group:
        scaled = []
        for i, block in enumerate(blocks):
            pivot = jnp.sum(jnp.where(lanes == rows + 8 * i, block, 0.0), axis=1, keepdims=True)
            scaled.append(block * lax.rsqrt(pivot))
        full = jnp.concatenate(scaled, axis=0)
        keep = jnp.logical_or(iota((64, 128), 1) >= 64, iota((64, 128), 1) >= iota((64, 128), 0))
        result.append(jnp.where(keep, full, 0.0))
    return result


def small_step(gc, rayleigh, order, kept):
    r64, c64 = iota((64, 64), 0), iota((64, 64), 1)
    eye = (r64 == c64).astype(F32)
    order_col = jnp.sum(jnp.where(r64 == c64, order, 0).astype(F32), axis=1, keepdims=True).astype(jnp.int32)
    kept_col = jnp.sum(jnp.where(iota((32, 32), 0) == iota((32, 32), 1), kept, 0).astype(F32), axis=1, keepdims=True).astype(jnp.int32)
    select_order = (order_col == c64).astype(F32)
    select_kept = (kept_col == iota((32, 64), 1)).astype(F32)
    cross_t = gc[:, 64:]
    a1 = jnp.concatenate([gc[:, :64], eye], axis=1)
    a2 = jnp.concatenate([mm(cross_t, cross_t, NT), eye], axis=1)
    a1, a2 = eliminate([a1, a2])
    lower_t, lower_inv, cross_low = a1[:, :64], a1[:, 64:], a2[:, 64:]
    side = mm(lower_inv, rayleigh, NT)
    ordered = mm(select_order, jnp.concatenate([lower_t, side], axis=1))
    permuted_t = mm(ordered[:, 64:], ordered[:, :64], NT)
    a3 = jnp.concatenate([mm(permuted_t, permuted_t, NT), permuted_t], axis=1)
    cross_inv = mm(cross_low, mm(cross_low, cross_t), TN)
    cross_inv = cross_inv + mm(cross_inv, eye - mm(cross_t, cross_inv, TN))
    tail = jnp.concatenate([lower_inv, mm(lower_t, cross_inv)], axis=1)
    basis_t = eliminate([a3])[0][:, 64:]
    weight = jnp.where(r64 > c64, 1.0, jnp.where(r64 == c64, 0.5, 0.0))
    for _ in range(2):
        basis_t = basis_t - mm((mm(basis_t, basis_t, NT) - eye) * weight, basis_t)
    kept_t = mm(select_kept, basis_t)
    restarted = mm(mm(kept_t, permuted_t, NT), kept_t, NT)
    return mm(kept_t, tail), restarted


def rotation_blocks(rotation):
    high, low = split(rotation)
    zero = jnp.zeros((KEEP, 128), BF16)

    def both(part):
        right, left = part[:, :64], part[:, 64:]
        return [
            jnp.concatenate([right, right, zero], axis=1),
            jnp.concatenate([zero, left, left], axis=1),
        ]

    return jnp.concatenate(both(high) + both(low), axis=0)


def rotated(rotate, block):
    both = mm16(rotate, block)
    return both[:64] + both[64:]


def core_kernel(right_ref, left_ref, speed_hbm, rim_hbm, rayleigh_hbm, order_hbm, kept_hbm,
                new_ref, image_ref, speed_ref, restarted_ref, ang_ref, ax_ref,
                buf_ref, cells_ref, field_ref, acc_ref, edge_ref, part_ref, got_ref, sum_ref, ang_buf, ax_buf, raw_ref,
                near_ref, rim_ref, rayleigh_ref, order_ref, kept_ref, load_sem, small_sem, send_sem, recv_sem):
    small = [pltpu.make_async_copy(src, dst, small_sem.at[i]) for i, (src, dst) in enumerate((
        (speed_hbm, speed_ref), (rim_hbm, rim_ref), (rayleigh_hbm, rayleigh_ref), (order_hbm, order_ref), (kept_hbm, kept_ref)))]
    for copy in small:
        copy.start()
    refs = (right_ref, left_ref)
    sector, slab = lax.axis_index("sector"), lax.axis_index("slab")
    x, y, z, core = place(sector, slab)
    other = device(x, y, z, 1 - core)
    groups = (
        (x, [device(lax.rem(x + o, 4), y, z, core) for o in (1, 2, 3)]),
        (y, [device(x, lax.rem(y + o, 4), z, core) for o in (1, 2, 3)]),
        (z, [device(x, y, lax.rem(z + o, 4), core) for o in (1, 2, 3)]),
    )
    ang_to = ((lax.rem(sector + 15, 16), slab), (lax.rem(sector + 1, 16), slab))
    ax_to = ((sector, lax.rem(slab + 7, 8)), (sector, lax.rem(slab + 1, 8)))
    exists = (slab > 0, slab < 7)

    @pl.loop(0, CA)
    def _(i):
        a = lax.rem(CA - i, CA)
        for n in range(2):
            for t in range(CT):
                for j in range(2):
                    pltpu.make_async_copy(refs[n].at[:, a, j, t, :], buf_ref.at[a, t, n, j], load_sem.at[a]).start()

    barrier = pltpu.get_barrier_semaphore()
    for peer in [other] + [p for _, peers in groups for p in peers] + list(ang_to + ax_to):
        pl.semaphore_signal(barrier, inc=1, device_id=peer, device_id_type=MESH)

    def remote(src, dst, n, peer):
        return pltpu.make_async_remote_copy(
            src_ref=src, dst_ref=dst, send_sem=send_sem.at[n], recv_sem=recv_sem.at[n],
            device_id=peer, device_id_type=MESH)

    def early_copies(side):
        a = side * (CA - 1)
        copies = [remote(speed_ref.at[a], near_ref.at[1 - side], 13 + side, ax_to[side])]
        if EARLY:
            copies.append(remote(buf_ref.at[a, 0:EARLY], raw_ref.at[1 - side, 0:EARLY], 11 + side, ax_to[side]))
        return copies

    def later_copies(side):
        a = side * (CA - 1)
        if RAW == EARLY:
            return []
        return [remote(buf_ref.at[a, EARLY:RAW], raw_ref.at[1 - side, EARLY:RAW], 19 + side, ax_to[side])]

    for copy in small:
        copy.wait()
    acc_ref[...] = jnp.zeros_like(acc_ref)
    hot = (iota((CR, CR), 0) == rim_ref[...]).astype(BF16)

    @pl.loop(0, CA)
    def _(i):
        a = lax.rem(CA - i, CA)
        pltpu.make_async_copy(buf_ref.at[a], buf_ref.at[a], load_sem.at[a]).wait()
        for side in range(2):
            @pl.when(i == side)
            def _():
                if side == 0:
                    pl.semaphore_wait(barrier, 14)
                if True:
                    @pl.when(exists[side])
                    def _():
                        for copy in early_copies(side):
                            copy.start()

        columns = []
        for t in range(CT):
            for j in range(2):
                columns.append(stacked(buf_ref[a, t, 0, j], buf_ref[a, t, 1, j]))
        block = halves(columns)
        cells_ref[a] = block
        acc_ref[...] += mm16(block[:128], block, NT)
        for side, t in ((0, 0), (1, CT - 1)):
            scaled = halves([speed_ref[a, j, t:t + 1, :] * buf_ref[a, t, 1, j] for j in range(2)])
            edge = jnp.concatenate((block[:128, t * CR:(t + 1) * CR],) + split(scaled), axis=0)
            edge_ref[side, a] = mm16(edge, hot, NT if side else NN).astype(BF16)

    part_ref[...] = combined(acc_ref[...])

    def half(h):
        return pl.ds(pl.multiple_of(h * 32, 32), 32)

    copies = [remote(part_ref.at[half(1 - core)], got_ref.at[0, 0], 0, other)]
    copies[0].start()
    copies[0].wait_recv()
    mine, theirs = part_ref[half(core), :], got_ref[0, 0]
    total = mine + theirs
    n = 1
    for stage, (me, peers) in enumerate(groups):
        got_ref[stage + 1, me] = total
        sent = []
        for peer in peers:
            copy = remote(got_ref.at[stage + 1, me], got_ref.at[stage + 1, me], n, peer)
            copy.start()
            sent.append(copy)
            n += 1
        for copy in sent:
            copy.wait_recv()
        copies += sent
        total = (got_ref[stage + 1, 0] + got_ref[stage + 1, 1]) + (got_ref[stage + 1, 2] + got_ref[stage + 1, 3])
    sum_ref[half(core), :] = total
    copy = remote(sum_ref.at[half(core)], sum_ref.at[half(core)], n, other)
    copy.start()
    copy.wait_recv()
    copies.append(copy)

    for side in range(2):
        @pl.when(exists[side])
        def _():
            for copy in later_copies(side):
                copy.start()

    rotation, restarted = small_step(sum_ref[...] * (1.0 / CELLS), rayleigh_ref[...], order_ref[...], kept_ref[...])
    restarted_ref[...] = restarted
    rotate = rotation_blocks(rotation)

    for side in range(2):
        @pl.loop(0, CA)
        def _(a):
            ang_buf[side, a] = rotated(rotate, edge_ref[side, a])
        copy = remote(ang_buf.at[side], ang_ref.at[1 - side], 15 + side, ang_to[side])
        copy.start()
        copies.append(copy)
    ang_copies = copies[-2:]

    def speed_row(ref, t):
        return halves([ref[0, pl.ds(t, 1), :], ref[1, pl.ds(t, 1), :]])

    def ax_copy(side):
        return remote(ax_buf.at[side], ax_ref.at[1 - side, RAW:], 17 + side, ax_to[side])

    if RAW < CT:
        for side in range(2):
            a = side * (CA - 1)
            for t in range(RAW, CT):
                value = rotated(rotate, cells_ref[a, :, t * CR:(t + 1) * CR])
                ax_buf[side, t - RAW, 0:KEEP] = value[:KEEP]
                ax_buf[side, t - RAW, KEEP:] = value[KEEP:] * speed_row(speed_ref.at[a], t)

            @pl.when(exists[side])
            def _():
                ax_copy(side).start()

    @pl.loop(0, CA)
    def _(a):
        for t in range(CT):
            value = rotated(rotate, cells_ref[a, :, t * CR:(t + 1) * CR])
            for j in range(2):
                part = value[:, j * 128:(j + 1) * 128]
                new_ref[a, t, j] = part
                field_ref[a, t, j, 0:KEEP] = part[:KEEP]
                field_ref[a, t, j, KEEP:] = part[KEEP:] * speed_ref[a, j, t:t + 1, :]

    @pl.loop(0, CA)
    def _(a):
        lanes = iota((64, 128), 1)
        below, above = jnp.maximum(a - 1, 0), jnp.minimum(a + 1, CA - 1)
        has_below, has_above = (a > 0).astype(F32), (a < CA - 1).astype(F32)
        for t in range(CT):
            mid = [field_ref[a, t, j] for j in range(2)]
            up = [pltpu.roll(m, 1, 1) for m in mid]
            down = [pltpu.roll(m, 127, 1) for m in mid]
            behind = [jnp.where(lanes == 0, 0.0, up[0]), jnp.where(lanes == 0, up[0], up[1])]
            ahead = [jnp.where(lanes == 127, down[1], down[0]), jnp.where(lanes == 127, 0.0, down[1])]
            for j in range(2):
                total = field_ref[below, t, j] * has_below + field_ref[above, t, j] * has_above + behind[j] + ahead[j]
                if t > 0:
                    total = total + field_ref[a, t - 1, j]
                if t < CT - 1:
                    total = total + field_ref[a, t + 1, j]
                applied = 6.0 * mid[j] - total
                image_ref[a, t, j, 0:KEEP] = applied[:KEEP] * speed_ref[a, j, t:t + 1, :] - mid[j][:KEEP]
                image_ref[a, t, j, KEEP:] = applied[KEEP:] - new_ref[a, t, j, KEEP:]

    for side in range(2):
        @pl.when(exists[side])
        def _():
            for copy in early_copies(1 - side) + later_copies(1 - side):
                copy.wait_recv()

            @pl.loop(0, RAW)
            def _(t):
                block = stacked(halves([raw_ref[side, t, 0, 0], raw_ref[side, t, 0, 1]]),
                                halves([raw_ref[side, t, 1, 0], raw_ref[side, t, 1, 1]]))
                value = rotated(rotate, block)
                ax_ref[side, t, 0:KEEP] = value[:KEEP]
                ax_ref[side, t, KEEP:] = value[KEEP:] * speed_row(near_ref.at[side], t)

    for side in range(2):
        ang_copies[1 - side].wait_recv()

        @pl.when(exists[side])
        def _():
            if RAW < CT:
                ax_copy(1 - side).wait_recv()
                ax_copy(side).wait_send()
            for copy in early_copies(side) + later_copies(side):
                copy.wait_send()
    for copy in copies:
        copy.wait_send()


def core_step(right, left, speed, rim, rayleigh, order, kept):
    vmem = pl.BlockSpec(memory_space=pltpu.VMEM)
    main = pl.BlockSpec(memory_space=pltpu.HBM)
    sent = max(CT - RAW, 1)
    inputs = [pltpu.with_memory_space_constraint(v, pltpu.HBM) for v in (right, left, speed, rim, rayleigh, order, kept)]
    return pl.pallas_call(
        core_kernel,
        in_specs=[main] * 7,
        out_specs=[vmem] * 6,
        out_shape=[
            pltpu.VMEM((CA, CT, 2, 64, 128), F32),
            pltpu.VMEM((CA, CT, 2, 64, 128), F32),
            pltpu.VMEM((CA, 2, CT, 128), F32),
            pltpu.VMEM((KEEP, KEEP), F32),
            pltpu.VMEM((2, CA, 64, CR), F32),
            pltpu.VMEM((2, CT, 64, CR), F32),
        ],
        scratch_shapes=[
            pltpu.VMEM((CA, CT, 2, 2, 64, 128), F32),
            pltpu.VMEM((CA, 256, CT * CR), BF16),
            pltpu.VMEM((CA, CT, 2, 64, 128), F32),
            pltpu.VMEM((128, 256), F32),
            pltpu.VMEM((2, CA, 256, CR), BF16),
            pltpu.VMEM((64, 128), F32),
            pltpu.VMEM((4, 4, 32, 128), F32),
            pltpu.VMEM((64, 128), F32),
            pltpu.VMEM((2, CA, 64, CR), F32),
            pltpu.VMEM((2, sent, 64, CR), F32),
            pltpu.VMEM((2, RAW, 2, 2, 64, 128), F32),
            pltpu.VMEM((2, 2, CT, 128), F32),
            pltpu.VMEM((1, CR), jnp.int32),
            pltpu.VMEM((K, K), F32),
            pltpu.VMEM((1, K), jnp.int32),
            pltpu.VMEM((1, KEEP), jnp.int32),
            pltpu.SemaphoreType.DMA((CA,)),
            pltpu.SemaphoreType.DMA((5,)),
            pltpu.SemaphoreType.DMA((21,)),
            pltpu.SemaphoreType.DMA((21,)),
        ],
        compiler_params=pltpu.CompilerParams(collective_id=0, has_side_effects=True, vmem_limit_bytes=44 << 20),
        name="core",
    )(*inputs)


def finish_kernel(new_ref, image_ref, speed_ref, restarted_in, ang_ref, ax_ref, new_right_ref, new_left_ref,
                  right_image_ref, left_image_ref, restarted_ref, fix_ref, sem):
    slab = lax.axis_index("slab")
    outs = (new_right_ref, new_left_ref, right_image_ref, left_image_ref)

    def send(n, src, a, t):
        for j in range(2):
            low = (n % 2) * KEEP
            pltpu.make_async_copy(src.at[t, j, low:low + KEEP], outs[n].at[:, a, j, t, :], sem.at[n]).start()

    @pl.loop(0, CA)
    def _(a):
        for t in range(CT):
            send(0, new_ref.at[a], a, t)
            send(1, new_ref.at[a], a, t)

    @pl.loop(1, CA - 1)
    def _(a):
        for t in range(1, CT - 1):
            send(2, image_ref.at[a], a, t)
            send(3, image_ref.at[a], a, t)

    @pl.loop(0, CA)
    def _(a):
        def fix(t):
            for j in range(2):
                lanes = slice(j * 128, (j + 1) * 128)
                halo = jnp.zeros((64, 128), F32)
                if t == 0:
                    halo = halo + ang_ref[0, a, :, lanes]
                if t == CT - 1:
                    halo = halo + ang_ref[1, a, :, lanes]
                halo = halo + jnp.where(jnp.logical_and(a == 0, slab > 0), ax_ref[0, t, :, lanes], 0.0)
                halo = halo + jnp.where(jnp.logical_and(a == CA - 1, slab < 7), ax_ref[1, t, :, lanes], 0.0)
                value = image_ref[a, t, j]
                fix_ref[a, t, j, 0:KEEP] = value[:KEEP] - halo[:KEEP] * speed_ref[a, j, t:t + 1, :]
                fix_ref[a, t, j, KEEP:] = value[KEEP:] - halo[KEEP:]
            send(2, fix_ref.at[a], a, t)
            send(3, fix_ref.at[a], a, t)

        for t in (0, CT - 1):
            fix(t)

        @pl.when(jnp.logical_or(a == 0, a == CA - 1))
        def _():
            for t in range(1, CT - 1):
                fix(t)

    restarted_ref[...] = restarted_in[...]
    for n in range(4):
        pltpu.make_async_copy(outs[n], outs[n], sem.at[n]).wait()


def finish(*arrays):
    vmem = pl.BlockSpec(memory_space=pltpu.VMEM)
    main = pl.BlockSpec(memory_space=pltpu.HBM)
    kept = jax.ShapeDtypeStruct((KEEP, CA, 2, CT, 128), F32)
    return pl.pallas_call(
        finish_kernel,
        in_specs=[vmem] * 6,
        out_specs=[main] * 4 + [vmem],
        out_shape=[kept] * 4 + [jax.ShapeDtypeStruct((KEEP, KEEP), F32)],
        scratch_shapes=[pltpu.VMEM((CA, CT, 2, 64, 128), F32), pltpu.SemaphoreType.DMA((4,))],
        compiler_params=pltpu.CompilerParams(vmem_limit_bytes=10 << 20),
        name="finish",
    )(*[pltpu.with_memory_space_constraint(v, pltpu.VMEM) for v in arrays])


def tiles(array):
    return array.reshape(array.shape[0], CT, CA, 2, 128).transpose(0, 2, 3, 1, 4)


def local(right_basis, left_basis, speed_squared, rayleigh, schur_order, kept_index, rim_map):
    right, left, speed = tiles(right_basis), tiles(left_basis), tiles(speed_squared[None])[0]
    *outs, restarted = finish(*core_step(
        right, left, speed, rim_map.reshape(1, CR), rayleigh, schur_order.reshape(1, K), kept_index.reshape(1, KEEP)))
    shape = (KEEP, CT, CA, CR)
    return tuple(o.transpose(0, 3, 1, 2, 4).reshape(shape) for o in outs) + (restarted,)


def solution(mesh):
    fields = P(None, "sector", "slab", None)
    return jax.shard_map(
        local,
        mesh=mesh,
        in_specs=(fields, fields, P("sector", "slab", None), P(), P(), P(), P()),
        out_specs=(fields, fields, fields, fields, P()),
        check_vma=False,
    )
```

```python
import jax
import jax.numpy as jnp
from jax import lax
from jax.experimental import pallas as pl
from jax.experimental.pallas import tpu as pltpu
from jax.sharding import PartitionSpec as P

MESH = pl.DeviceIdType.MESH
NN = (((1,), (0,)), ((), ()))
NT = (((1,), (1,)), ((), ()))
TN = (((0,), (0,)), ((), ()))
F32 = jnp.float32
BF16 = jnp.bfloat16
K, KEEP, CT, CA, CR = 64, 32, 8, 12, 256
CELLS = 3145728
SENT = (6, 6, 6, 6, 6, 6, 8)
RAW = SENT[-1] // 2


def mm(a, b, dims=NN):
    return lax.dot_general(a, b, dims, precision=lax.Precision.HIGHEST, preferred_element_type=F32)


def mm16(a, b, dims=NN):
    return lax.dot_general(a, b, dims, preferred_element_type=F32)


def iota(shape, dim):
    return lax.broadcasted_iota(jnp.int32, shape, dim)


def split(x):
    high = x.astype(BF16)
    return high, (x - high.astype(F32)).astype(BF16)


def stacked(right, left):
    return jnp.concatenate(split(right) + split(left), axis=0)


def halves(pair):
    return jnp.concatenate(pair, axis=1)


def place(sector, slab):
    return sector // 4, slab // 2, (slab % 2) * 2 + (sector // 2) % 2, sector % 2


def device(x, y, z, core):
    return (x * 4 + (z % 2) * 2 + core, y * 2 + z // 2)


def combined(part):
    top = part[:64] + part[64:]
    gram, cross = top[:, :128], top[:, 128:]
    gram, cross = gram + pltpu.roll(gram, 64, 1), cross + pltpu.roll(cross, 64, 1)
    return jnp.where(iota((64, 128), 1) < 64, gram, cross)


def pivots(group, first):
    rows = iota((8, 128), 0)
    top = first // 8
    states = []
    for blocks in group:
        columns = [[jnp.broadcast_to(blocks[i][:, first + j:first + j + 1], (8, 128)) for i in range(top, 8)] for j in range(8)]
        corner = [[columns[j][0][i:i + 1, :] for j in range(8)] for i in range(8)]
        states.append((columns, corner, [blocks[top][i:i + 1, :] for i in range(8)], []))
    for j in range(8):
        for columns, corner, lead, scaled in states:
            inverse = 1.0 / corner[j][j]
            scaled.append(lead[j] * inverse)
            for m in range(j + 1, 8):
                factor = corner[m][j] * inverse
                for i in range(m, 8):
                    corner[i][m] = corner[i][m] - corner[i][j] * factor
                lead[m] = lead[m] - corner[m][j] * scaled[j]
                columns[m] = [c - d * factor for c, d in zip(columns[m], columns[j])]
    result = []
    for blocks, (columns, _, _, scaled) in zip(group, states):
        blocks = list(blocks)
        for i in range(top, 8):
            for j in range(8):
                column = columns[j][i - top]
                if i == top:
                    column = jnp.where(rows > j, column, 0.0)
                blocks[i] = blocks[i] - column * scaled[j]
        result.append(blocks)
    return result


def eliminate(arrays):
    rows, lanes = iota((8, 128), 0), iota((8, 128), 1)
    group = [[a[8 * i:8 * i + 8, :] for i in range(8)] for a in arrays]
    for first in range(0, 64, 8):
        group = pivots(group, first)
    result = []
    for blocks in group:
        scaled = []
        for i, block in enumerate(blocks):
            pivot = jnp.sum(jnp.where(lanes == rows + 8 * i, block, 0.0), axis=1, keepdims=True)
            scaled.append(block * lax.rsqrt(pivot))
        full = jnp.concatenate(scaled, axis=0)
        keep = jnp.logical_or(iota((64, 128), 1) >= 64, iota((64, 128), 1) >= iota((64, 128), 0))
        result.append(jnp.where(keep, full, 0.0))
    return result


def small_step(gc, rayleigh, order, kept):
    r64, c64 = iota((64, 64), 0), iota((64, 64), 1)
    eye = (r64 == c64).astype(F32)
    order_col = jnp.sum(jnp.where(r64 == c64, order, 0).astype(F32), axis=1, keepdims=True).astype(jnp.int32)
    kept_col = jnp.sum(jnp.where(iota((32, 32), 0) == iota((32, 32), 1), kept, 0).astype(F32), axis=1, keepdims=True).astype(jnp.int32)
    select_order = (order_col == c64).astype(F32)
    select_kept = (kept_col == iota((32, 64), 1)).astype(F32)
    cross_t = gc[:, 64:]
    a1 = jnp.concatenate([gc[:, :64], eye], axis=1)
    a2 = jnp.concatenate([mm(cross_t, cross_t, NT), eye], axis=1)
    a1, a2 = eliminate([a1, a2])
    lower_t, lower_inv, cross_low = a1[:, :64], a1[:, 64:], a2[:, 64:]
    side = mm(lower_inv, rayleigh, NT)
    ordered = mm(select_order, jnp.concatenate([lower_t, side], axis=1))
    permuted_t = mm(ordered[:, 64:], ordered[:, :64], NT)
    a3 = jnp.concatenate([mm(permuted_t, permuted_t, NT), permuted_t], axis=1)
    cross_inv = mm(cross_low, mm(cross_low, cross_t), TN)
    cross_inv = cross_inv + mm(cross_inv, eye - mm(cross_t, cross_inv, TN))
    tail = jnp.concatenate([lower_inv, mm(lower_t, cross_inv)], axis=1)
    basis_t = eliminate([a3])[0][:, 64:]
    weight = jnp.where(r64 > c64, 1.0, jnp.where(r64 == c64, 0.5, 0.0))
    basis_t = basis_t - mm((mm(basis_t, basis_t, NT) - eye) * weight, basis_t)
    change = (mm(basis_t, basis_t, NT) - eye) * weight
    chosen = select_kept - mm(select_kept, change)
    kept_t = mm(chosen, basis_t)
    restarted = mm(mm(kept_t, permuted_t, NT), kept_t, NT)
    return mm(chosen, mm(basis_t, tail)), restarted


def rotation_blocks(rotation):
    high, low = split(rotation)
    zero = jnp.zeros((KEEP, 128), BF16)

    def both(part):
        right, left = part[:, :64], part[:, 64:]
        return [
            jnp.concatenate([right, right, zero], axis=1),
            jnp.concatenate([zero, left, left], axis=1),
        ]

    return jnp.concatenate(both(high) + both(low), axis=0)


def rotated(rotate, block):
    both = mm16(rotate, block)
    return both[:64] + both[64:]


def core_kernel(right_ref, left_ref, speed_hbm, rim_hbm, rayleigh_hbm, order_hbm, kept_hbm,
                new_ref, image_ref, speed_ref, restarted_ref, ang_ref, ax_ref,
                buf_ref, cells_ref, field_ref, acc_ref, edge_ref, part_ref, got_ref, sum_ref, ang_buf, ax_buf, raw_ref,
                near_ref, rim_ref, rayleigh_ref, order_ref, kept_ref, load_sem, small_sem, send_sem, recv_sem):
    small = [pltpu.make_async_copy(src, dst, small_sem.at[i]) for i, (src, dst) in enumerate((
        (speed_hbm, speed_ref), (rim_hbm, rim_ref), (rayleigh_hbm, rayleigh_ref), (order_hbm, order_ref), (kept_hbm, kept_ref)))]
    for copy in small:
        copy.start()
    refs = (right_ref, left_ref)
    sector, slab = lax.axis_index("sector"), lax.axis_index("slab")
    x, y, z, core = place(sector, slab)
    other = device(x, y, z, 1 - core)
    groups = (
        (x, [device(lax.rem(x + o, 4), y, z, core) for o in (1, 2, 3)]),
        (y, [device(x, lax.rem(y + o, 4), z, core) for o in (1, 2, 3)]),
        (z, [device(x, y, lax.rem(z + o, 4), core) for o in (1, 2, 3)]),
    )
    ang_to = ((lax.rem(sector + 15, 16), slab), (lax.rem(sector + 1, 16), slab))
    ax_to = ((sector, lax.rem(slab + 7, 8)), (sector, lax.rem(slab + 1, 8)))
    exists = (slab > 0, slab < 7)

    @pl.loop(0, CA)
    def _(i):
        a = lax.rem(CA - i, CA)
        for n in range(2):
            for t in range(CT):
                for j in range(2):
                    pltpu.make_async_copy(refs[n].at[:, a, j, t, :], buf_ref.at[a, 2 * t + n, j], load_sem.at[a]).start()

    barrier = pltpu.get_barrier_semaphore()
    for peer in [other] + [p for _, peers in groups for p in peers] + list(ang_to + ax_to):
        pl.semaphore_signal(barrier, inc=1, device_id=peer, device_id_type=MESH)

    def remote(src, dst, n, peer):
        return pltpu.make_async_remote_copy(
            src_ref=src, dst_ref=dst, send_sem=send_sem.at[n], recv_sem=recv_sem.at[n],
            device_id=peer, device_id_type=MESH)

    def near_copy(side):
        return remote(speed_ref.at[side * (CA - 1)], near_ref.at[1 - side], 11 + side, ax_to[side])

    def raw_copies(side, stage=None):
        a = side * (CA - 1)
        copies = []
        for i in range(len(SENT)):
            units = slice(SENT[i - 1] if i else 0, SENT[i])
            if units.start < units.stop and stage in (None, i):
                copies.append(remote(buf_ref.at[a, units], raw_ref.at[1 - side, units], 19 + 2 * i + side, ax_to[side]))
        return copies

    def send_raw(stage):
        if stage and SENT[stage] == SENT[stage - 1]:
            return
        for side in range(2):
            @pl.when(exists[side])
            def _():
                for copy in raw_copies(side, stage):
                    copy.start()

    for copy in small:
        copy.wait()
    acc_ref[...] = jnp.zeros_like(acc_ref)
    hot = (iota((CR, CR), 0) == rim_ref[...]).astype(BF16)

    @pl.loop(0, CA)
    def _(i):
        a = lax.rem(CA - i, CA)
        pltpu.make_async_copy(buf_ref.at[a], buf_ref.at[a], load_sem.at[a]).wait()
        for side in range(2):
            @pl.when(i == side)
            def _():
                if side == 0:
                    pl.semaphore_wait(barrier, 14)
                if True:
                    @pl.when(exists[side])
                    def _():
                        for copy in [near_copy(side)] + raw_copies(side, 0):
                            copy.start()

        columns = []
        for t in range(CT):
            for j in range(2):
                columns.append(stacked(buf_ref[a, 2 * t, j], buf_ref[a, 2 * t + 1, j]))
        block = halves(columns)
        cells_ref[a] = block
        acc_ref[...] += mm16(block[:128], block, NT)

    part_ref[...] = combined(acc_ref[...])

    def edges(side):
        t = side * (CT - 1)

        @pl.loop(0, CA)
        def _(a):
            scaled = halves([speed_ref[a, j, t:t + 1, :] * buf_ref[a, 2 * t + 1, j] for j in range(2)])
            edge = jnp.concatenate((cells_ref[a, 0:128, t * CR:(t + 1) * CR],) + split(scaled), axis=0)
            edge_ref[side, a] = mm16(edge, hot, NT if side else NN).astype(BF16)

    def half(h):
        return pl.ds(pl.multiple_of(h * 32, 32), 32)

    copies = [remote(part_ref.at[half(1 - core)], got_ref.at[0, 0], 0, other)]
    copies[0].start()
    send_raw(1)
    edges(0)
    copies[0].wait_recv()
    mine, theirs = part_ref[half(core), :], got_ref[0, 0]
    total = mine + theirs
    n = 1
    for stage, (me, peers) in enumerate(groups):
        got_ref[stage + 1, me] = total
        sent = []
        for peer in peers:
            copy = remote(got_ref.at[stage + 1, me], got_ref.at[stage + 1, me], n, peer)
            copy.start()
            sent.append(copy)
            n += 1
        send_raw(stage + 2)
        if stage == 0:
            edges(1)
        for copy in sent:
            copy.wait_recv()
        copies += sent
        total = (got_ref[stage + 1, 0] + got_ref[stage + 1, 1]) + (got_ref[stage + 1, 2] + got_ref[stage + 1, 3])
    sum_ref[half(core), :] = total
    copy = remote(sum_ref.at[half(core)], sum_ref.at[half(core)], n, other)
    copy.start()
    send_raw(5)
    copy.wait_recv()
    copies.append(copy)

    send_raw(6)
    rotation, restarted = small_step(sum_ref[...] * (1.0 / CELLS), rayleigh_ref[...], order_ref[...], kept_ref[...])
    restarted_ref[...] = restarted
    rotate = rotation_blocks(rotation)

    def speed_row(ref, t):
        return halves([ref[0, pl.ds(t, 1), :], ref[1, pl.ds(t, 1), :]])

    def ax_copy(side):
        return remote(ax_buf.at[side], ax_ref.at[1 - side, RAW:], 17 + side, ax_to[side])

    if RAW < CT:
        for side in range(2):
            a = side * (CA - 1)
            for t in range(RAW, CT):
                value = rotated(rotate, cells_ref[a, :, t * CR:(t + 1) * CR])
                ax_buf[side, t - RAW, 0:KEEP] = value[:KEEP]
                ax_buf[side, t - RAW, KEEP:] = value[KEEP:] * speed_row(speed_ref.at[a], t)

            @pl.when(exists[side])
            def _():
                ax_copy(side).start()

    for side in range(2):
        @pl.loop(0, CA)
        def _(a):
            ang_buf[side, a] = rotated(rotate, edge_ref[side, a])
        copy = remote(ang_buf.at[side], ang_ref.at[1 - side], 15 + side, ang_to[side])
        copy.start()
        copies.append(copy)
    ang_copies = copies[-2:]

    @pl.loop(0, CA)
    def _(a):
        for t in range(CT):
            value = rotated(rotate, cells_ref[a, :, t * CR:(t + 1) * CR])
            for j in range(2):
                part = value[:, j * 128:(j + 1) * 128]
                new_ref[a, t, j] = part
                field_ref[a, t, j, 0:KEEP] = part[:KEEP]
                field_ref[a, t, j, KEEP:] = part[KEEP:] * speed_ref[a, j, t:t + 1, :]

    @pl.loop(0, CA)
    def _(a):
        lanes = iota((64, 128), 1)
        below, above = jnp.maximum(a - 1, 0), jnp.minimum(a + 1, CA - 1)
        has_below, has_above = (a > 0).astype(F32), (a < CA - 1).astype(F32)
        for t in range(CT):
            mid = [field_ref[a, t, j] for j in range(2)]
            up = [pltpu.roll(m, 1, 1) for m in mid]
            down = [pltpu.roll(m, 127, 1) for m in mid]
            behind = [jnp.where(lanes == 0, 0.0, up[0]), jnp.where(lanes == 0, up[0], up[1])]
            ahead = [jnp.where(lanes == 127, down[1], down[0]), jnp.where(lanes == 127, 0.0, down[1])]
            for j in range(2):
                total = field_ref[below, t, j] * has_below + field_ref[above, t, j] * has_above + behind[j] + ahead[j]
                if t > 0:
                    total = total + field_ref[a, t - 1, j]
                if t < CT - 1:
                    total = total + field_ref[a, t + 1, j]
                applied = 6.0 * mid[j] - total
                image_ref[a, t, j, 0:KEEP] = applied[:KEEP] * speed_ref[a, j, t:t + 1, :] - mid[j][:KEEP]
                image_ref[a, t, j, KEEP:] = applied[KEEP:] - new_ref[a, t, j, KEEP:]

    for side in range(2):
        @pl.when(exists[side])
        def _():
            for copy in [near_copy(1 - side)] + raw_copies(1 - side):
                copy.wait_recv()

            @pl.loop(0, RAW)
            def _(t):
                block = stacked(halves([raw_ref[side, 2 * t, 0], raw_ref[side, 2 * t, 1]]),
                                halves([raw_ref[side, 2 * t + 1, 0], raw_ref[side, 2 * t + 1, 1]]))
                value = rotated(rotate, block)
                ax_ref[side, t, 0:KEEP] = value[:KEEP]
                ax_ref[side, t, KEEP:] = value[KEEP:] * speed_row(near_ref.at[side], t)

    for side in range(2):
        ang_copies[1 - side].wait_recv()

        @pl.when(exists[side])
        def _():
            if RAW < CT:
                ax_copy(1 - side).wait_recv()
                ax_copy(side).wait_send()
            for copy in [near_copy(side)] + raw_copies(side):
                copy.wait_send()
    for copy in copies:
        copy.wait_send()


def core_step(right, left, speed, rim, rayleigh, order, kept):
    vmem = pl.BlockSpec(memory_space=pltpu.VMEM)
    main = pl.BlockSpec(memory_space=pltpu.HBM)
    sent = max(CT - RAW, 1)
    inputs = [pltpu.with_memory_space_constraint(v, pltpu.HBM) for v in (right, left, speed, rim, rayleigh, order, kept)]
    return pl.pallas_call(
        core_kernel,
        in_specs=[main] * 7,
        out_specs=[vmem] * 6,
        out_shape=[
            pltpu.VMEM((CA, CT, 2, 64, 128), F32),
            pltpu.VMEM((CA, CT, 2, 64, 128), F32),
            pltpu.VMEM((CA, 2, CT, 128), F32),
            pltpu.VMEM((KEEP, KEEP), F32),
            pltpu.VMEM((2, CA, 64, CR), F32),
            pltpu.VMEM((2, CT, 64, CR), F32),
        ],
        scratch_shapes=[
            pltpu.VMEM((CA, 2 * CT, 2, 64, 128), F32),
            pltpu.VMEM((CA, 256, CT * CR), BF16),
            pltpu.VMEM((CA, CT, 2, 64, 128), F32),
            pltpu.VMEM((128, 256), F32),
            pltpu.VMEM((2, CA, 256, CR), BF16),
            pltpu.VMEM((64, 128), F32),
            pltpu.VMEM((4, 4, 32, 128), F32),
            pltpu.VMEM((64, 128), F32),
            pltpu.VMEM((2, CA, 64, CR), F32),
            pltpu.VMEM((2, sent, 64, CR), F32),
            pltpu.VMEM((2, 2 * RAW, 2, 64, 128), F32),
            pltpu.VMEM((2, 2, CT, 128), F32),
            pltpu.VMEM((1, CR), jnp.int32),
            pltpu.VMEM((K, K), F32),
            pltpu.VMEM((1, K), jnp.int32),
            pltpu.VMEM((1, KEEP), jnp.int32),
            pltpu.SemaphoreType.DMA((CA,)),
            pltpu.SemaphoreType.DMA((5,)),
            pltpu.SemaphoreType.DMA((33,)),
            pltpu.SemaphoreType.DMA((33,)),
        ],
        compiler_params=pltpu.CompilerParams(collective_id=0, has_side_effects=True, vmem_limit_bytes=44 << 20),
        name="core",
    )(*inputs)


def finish_kernel(new_ref, image_ref, speed_ref, restarted_in, ang_ref, ax_ref, new_right_ref, new_left_ref,
                  right_image_ref, left_image_ref, restarted_ref, fix_ref, sem):
    slab = lax.axis_index("slab")
    outs = (new_right_ref, new_left_ref, right_image_ref, left_image_ref)

    def send(n, src, a, t):
        for j in range(2):
            low = (n % 2) * KEEP
            pltpu.make_async_copy(src.at[t, j, low:low + KEEP], outs[n].at[:, a, j, t, :], sem.at[n]).start()

    @pl.loop(0, CA)
    def _(a):
        for t in range(CT):
            send(0, new_ref.at[a], a, t)
            send(1, new_ref.at[a], a, t)

    @pl.loop(1, CA - 1)
    def _(a):
        for t in range(1, CT - 1):
            send(2, image_ref.at[a], a, t)
            send(3, image_ref.at[a], a, t)

    @pl.loop(0, CA)
    def _(a):
        def fix(t):
            for j in range(2):
                lanes = slice(j * 128, (j + 1) * 128)
                halo = jnp.zeros((64, 128), F32)
                if t == 0:
                    halo = halo + ang_ref[0, a, :, lanes]
                if t == CT - 1:
                    halo = halo + ang_ref[1, a, :, lanes]
                halo = halo + jnp.where(jnp.logical_and(a == 0, slab > 0), ax_ref[0, t, :, lanes], 0.0)
                halo = halo + jnp.where(jnp.logical_and(a == CA - 1, slab < 7), ax_ref[1, t, :, lanes], 0.0)
                value = image_ref[a, t, j]
                fix_ref[a, t, j, 0:KEEP] = value[:KEEP] - halo[:KEEP] * speed_ref[a, j, t:t + 1, :]
                fix_ref[a, t, j, KEEP:] = value[KEEP:] - halo[KEEP:]
            send(2, fix_ref.at[a], a, t)
            send(3, fix_ref.at[a], a, t)

        for t in (0, CT - 1):
            fix(t)

        @pl.when(jnp.logical_or(a == 0, a == CA - 1))
        def _():
            for t in range(1, CT - 1):
                fix(t)

    restarted_ref[...] = restarted_in[...]
    for n in range(4):
        pltpu.make_async_copy(outs[n], outs[n], sem.at[n]).wait()


def finish(*arrays):
    vmem = pl.BlockSpec(memory_space=pltpu.VMEM)
    main = pl.BlockSpec(memory_space=pltpu.HBM)
    kept = jax.ShapeDtypeStruct((KEEP, CA, 2, CT, 128), F32)
    return pl.pallas_call(
        finish_kernel,
        in_specs=[vmem] * 6,
        out_specs=[main] * 4 + [vmem],
        out_shape=[kept] * 4 + [jax.ShapeDtypeStruct((KEEP, KEEP), F32)],
        scratch_shapes=[pltpu.VMEM((CA, CT, 2, 64, 128), F32), pltpu.SemaphoreType.DMA((4,))],
        compiler_params=pltpu.CompilerParams(vmem_limit_bytes=10 << 20),
        name="finish",
    )(*[pltpu.with_memory_space_constraint(v, pltpu.VMEM) for v in arrays])


def tiles(array):
    return array.reshape(array.shape[0], CT, CA, 2, 128).transpose(0, 2, 3, 1, 4)


def local(right_basis, left_basis, speed_squared, rayleigh, schur_order, kept_index, rim_map):
    right, left, speed = tiles(right_basis), tiles(left_basis), tiles(speed_squared[None])[0]
    *outs, restarted = finish(*core_step(
        right, left, speed, rim_map.reshape(1, CR), rayleigh, schur_order.reshape(1, K), kept_index.reshape(1, KEEP)))
    shape = (KEEP, CT, CA, CR)
    return tuple(o.transpose(0, 3, 1, 2, 4).reshape(shape) for o in outs) + (restarted,)


def solution(mesh):
    fields = P(None, "sector", "slab", None)
    return jax.shard_map(
        local,
        mesh=mesh,
        in_specs=(fields, fields, P("sector", "slab", None), P(), P(), P(), P()),
        out_specs=(fields, fields, fields, fields, P()),
        check_vma=False,
    )
```

```python
import jax
import jax.numpy as jnp
from jax import lax
from jax.experimental import pallas as pl
from jax.experimental.pallas import tpu as pltpu
from jax.sharding import PartitionSpec as P

MESH = pl.DeviceIdType.MESH
NN = (((1,), (0,)), ((), ()))
NT = (((1,), (1,)), ((), ()))
TN = (((0,), (0,)), ((), ()))
F32 = jnp.float32
BF16 = jnp.bfloat16
K, KEEP, CT, CA, CR = 64, 32, 8, 12, 256
CELLS = 3145728
SENT = (6, 8)
RAW = SENT[-1] // 2


def mm(a, b, dims=NN):
    return lax.dot_general(a, b, dims, precision=lax.Precision.HIGHEST, preferred_element_type=F32)


def mm16(a, b, dims=NN):
    return lax.dot_general(a, b, dims, preferred_element_type=F32)


def iota(shape, dim):
    return lax.broadcasted_iota(jnp.int32, shape, dim)


def split(x):
    high = x.astype(BF16)
    return high, (x - high.astype(F32)).astype(BF16)


def stacked(right, left):
    return jnp.concatenate(split(right) + split(left), axis=0)


def halves(pair):
    return jnp.concatenate(pair, axis=1)


def place(sector, slab):
    return sector // 4, slab // 2, (slab % 2) * 2 + (sector // 2) % 2, sector % 2


def device(x, y, z, core):
    return (x * 4 + (z % 2) * 2 + core, y * 2 + z // 2)


def combined(part):
    top = part[:64] + part[64:]
    gram, cross = top[:, :128], top[:, 128:]
    gram, cross = gram + pltpu.roll(gram, 64, 1), cross + pltpu.roll(cross, 64, 1)
    return jnp.where(iota((64, 128), 1) < 64, gram, cross)


def pivots(group, first):
    rows = iota((8, 128), 0)
    top = first // 8
    states = []
    for blocks in group:
        columns = [[jnp.broadcast_to(blocks[i][:, first + j:first + j + 1], (8, 128)) for i in range(top, 8)] for j in range(8)]
        corner = [[columns[j][0][i:i + 1, :] for j in range(8)] for i in range(8)]
        states.append((columns, corner, [blocks[top][i:i + 1, :] for i in range(8)], []))
    for j in range(8):
        for columns, corner, lead, scaled in states:
            inverse = 1.0 / corner[j][j]
            scaled.append(lead[j] * inverse)
            for m in range(j + 1, 8):
                factor = corner[m][j] * inverse
                for i in range(m, 8):
                    corner[i][m] = corner[i][m] - corner[i][j] * factor
                lead[m] = lead[m] - corner[m][j] * scaled[j]
                columns[m] = [c - d * factor for c, d in zip(columns[m], columns[j])]
    result = []
    for blocks, (columns, _, _, scaled) in zip(group, states):
        blocks = list(blocks)
        for i in range(top, 8):
            for j in range(8):
                column = columns[j][i - top]
                if i == top:
                    column = jnp.where(rows > j, column, 0.0)
                blocks[i] = blocks[i] - column * scaled[j]
        result.append(blocks)
    return result


def eliminate(arrays):
    rows, lanes = iota((8, 128), 0), iota((8, 128), 1)
    group = [[a[8 * i:8 * i + 8, :] for i in range(8)] for a in arrays]
    for first in range(0, 64, 8):
        group = pivots(group, first)
    result = []
    for blocks in group:
        scaled = []
        for i, block in enumerate(blocks):
            pivot = jnp.sum(jnp.where(lanes == rows + 8 * i, block, 0.0), axis=1, keepdims=True)
            scaled.append(block * lax.rsqrt(pivot))
        full = jnp.concatenate(scaled, axis=0)
        keep = jnp.logical_or(iota((64, 128), 1) >= 64, iota((64, 128), 1) >= iota((64, 128), 0))
        result.append(jnp.where(keep, full, 0.0))
    return result


def small_step(gc, rayleigh, order, kept):
    r64, c64 = iota((64, 64), 0), iota((64, 64), 1)
    eye = (r64 == c64).astype(F32)
    order_col = jnp.sum(jnp.where(r64 == c64, order, 0).astype(F32), axis=1, keepdims=True).astype(jnp.int32)
    kept_col = jnp.sum(jnp.where(iota((32, 32), 0) == iota((32, 32), 1), kept, 0).astype(F32), axis=1, keepdims=True).astype(jnp.int32)
    select_order = (order_col == c64).astype(F32)
    select_kept = (kept_col == iota((32, 64), 1)).astype(F32)
    cross_t = gc[:, 64:]
    a1 = jnp.concatenate([gc[:, :64], eye], axis=1)
    a2 = jnp.concatenate([mm(cross_t, cross_t, NT), eye], axis=1)
    a1, a2 = eliminate([a1, a2])
    lower_t, lower_inv, cross_low = a1[:, :64], a1[:, 64:], a2[:, 64:]
    side = mm(lower_inv, rayleigh, NT)
    ordered = mm(select_order, jnp.concatenate([lower_t, side], axis=1))
    permuted_t = mm(ordered[:, 64:], ordered[:, :64], NT)
    a3 = jnp.concatenate([mm(permuted_t, permuted_t, NT), permuted_t], axis=1)
    cross_inv = mm(cross_low, mm(cross_low, cross_t), TN)
    cross_inv = cross_inv + mm(cross_inv, eye - mm(cross_t, cross_inv, TN))
    tail = jnp.concatenate([lower_inv, mm(lower_t, cross_inv)], axis=1)
    basis_t = eliminate([a3])[0][:, 64:]
    weight = jnp.where(r64 > c64, 1.0, jnp.where(r64 == c64, 0.5, 0.0))
    basis_t = basis_t - mm((mm(basis_t, basis_t, NT) - eye) * weight, basis_t)
    change = (mm(basis_t, basis_t, NT) - eye) * weight
    chosen = select_kept - mm(select_kept, change)
    kept_t = mm(chosen, basis_t)
    restarted = mm(mm(kept_t, permuted_t, NT), kept_t, NT)
    return mm(chosen, mm(basis_t, tail)), restarted


def rotation_blocks(rotation):
    high, low = split(rotation)
    zero = jnp.zeros((KEEP, 128), BF16)

    def both(part):
        right, left = part[:, :64], part[:, 64:]
        return [
            jnp.concatenate([right, right, zero], axis=1),
            jnp.concatenate([zero, left, left], axis=1),
        ]

    return jnp.concatenate(both(high) + both(low), axis=0)


def rotated(rotate, block):
    both = mm16(rotate, block)
    return both[:64] + both[64:]


def core_kernel(right_ref, left_ref, speed_hbm, rim_hbm, rayleigh_hbm, order_hbm, kept_hbm,
                new_ref, image_ref, speed_ref, restarted_ref, ang_ref, ax_ref,
                buf_ref, cells_ref, field_ref, acc_ref, edge_ref, part_ref, row_ref, line_ref, column_ref, sum_ref, ang_buf, ax_buf, raw_ref,
                near_ref, rim_ref, rayleigh_ref, order_ref, kept_ref, load_sem, small_sem, send_sem, recv_sem):
    small = [pltpu.make_async_copy(src, dst, small_sem.at[i]) for i, (src, dst) in enumerate((
        (speed_hbm, speed_ref), (rim_hbm, rim_ref), (rayleigh_hbm, rayleigh_ref), (order_hbm, order_ref), (kept_hbm, kept_ref)))]
    for copy in small:
        copy.start()
    refs = (right_ref, left_ref)
    sector, slab = lax.axis_index("sector"), lax.axis_index("slab")
    x, y, z, core = place(sector, slab)
    lane, column = 2 * x + core, 2 * z + core

    def in_row(o):
        other = lax.rem(lane + o, 8)
        return lax.rem(other, 2), device(other // 2, y, z, lax.rem(other, 2))

    def in_line(o):
        return device(x, lax.rem(y + o, 4), z, core)

    def in_column(o):
        other = lax.rem(column + o, 8)
        return device(x, y, other // 2, lax.rem(other, 2))

    ang_to = ((lax.rem(sector + 15, 16), slab), (lax.rem(sector + 1, 16), slab))
    ax_to = ((sector, lax.rem(slab + 7, 8)), (sector, lax.rem(slab + 1, 8)))
    exists = (slab > 0, slab < 7)

    @pl.loop(0, CA)
    def _(i):
        a = lax.rem(CA - i, CA)
        for n in range(2):
            for t in range(CT):
                for j in range(2):
                    pltpu.make_async_copy(refs[n].at[:, a, j, t, :], buf_ref.at[a, 2 * t + n, j], load_sem.at[a]).start()

    barrier = pltpu.get_barrier_semaphore()
    for peer in ([in_row(o)[1] for o in range(1, 8)] + [in_line(o) for o in range(1, 4)]
                 + [in_column(o) for o in range(1, 8)] + list(ang_to + ax_to)):
        pl.semaphore_signal(barrier, inc=1, device_id=peer, device_id_type=MESH)

    def remote(src, dst, n, peer):
        return pltpu.make_async_remote_copy(
            src_ref=src, dst_ref=dst, send_sem=send_sem.at[n], recv_sem=recv_sem.at[n],
            device_id=peer, device_id_type=MESH)

    def near_copy(side):
        return remote(speed_ref.at[side * (CA - 1)], near_ref.at[1 - side], 11 + side, ax_to[side])

    def raw_copies(side, stage=None):
        a = side * (CA - 1)
        copies = []
        for i in range(len(SENT)):
            units = slice(SENT[i - 1] if i else 0, SENT[i])
            if units.start < units.stop and stage in (None, i):
                copies.append(remote(buf_ref.at[a, units], raw_ref.at[1 - side, units], 19 + 2 * i + side, ax_to[side]))
        return copies

    def send_raw(stage):
        if stage and SENT[stage] == SENT[stage - 1]:
            return
        for side in range(2):
            @pl.when(exists[side])
            def _():
                for copy in raw_copies(side, stage):
                    copy.start()

    for copy in small:
        copy.wait()
    acc_ref[...] = jnp.zeros_like(acc_ref)
    hot = (iota((CR, CR), 0) == rim_ref[...]).astype(BF16)

    @pl.loop(0, CA)
    def _(i):
        a = lax.rem(CA - i, CA)
        pltpu.make_async_copy(buf_ref.at[a], buf_ref.at[a], load_sem.at[a]).wait()
        for side in range(2):
            @pl.when(i == side)
            def _():
                if side == 0:
                    pl.semaphore_wait(barrier, 21)
                if True:
                    @pl.when(exists[side])
                    def _():
                        for copy in [near_copy(side)] + raw_copies(side, 0):
                            copy.start()

        columns = []
        for t in range(CT):
            for j in range(2):
                columns.append(stacked(buf_ref[a, 2 * t, j], buf_ref[a, 2 * t + 1, j]))
        block = halves(columns)
        cells_ref[a] = block
        acc_ref[...] += mm16(block[:128], block, NT)

    part_ref[...] = combined(acc_ref[...])

    def edges(side):
        t = side * (CT - 1)

        @pl.loop(0, CA)
        def _(a):
            scaled = halves([speed_ref[a, j, t:t + 1, :] * buf_ref[a, 2 * t + 1, j] for j in range(2)])
            edge = jnp.concatenate((cells_ref[a, 0:128, t * CR:(t + 1) * CR],) + split(scaled), axis=0)
            edge_ref[side, a] = mm16(edge, hot, NT if side else NN).astype(BF16)

    def half(h):
        return pl.ds(pl.multiple_of(h * 32, 32), 32)

    def summed(ref, *lead):
        parts = [ref[lead + (i,)] for i in range(ref.shape[len(lead)])]
        while len(parts) > 1:
            parts = [parts[i] + parts[i + 1] for i in range(0, len(parts), 2)]
        return parts[0]

    copies = []

    def spread(n, src, dst, peer):
        copy = remote(src, dst, n, peer)
        copy.start()
        copies.append(copy)

    for o in range(1, 8):
        side, peer = in_row(o)
        spread(o - 1, part_ref.at[half(side)], row_ref.at[lane], peer)
    row_ref[lane] = part_ref[half(core), :]
    edges(0)
    for copy in copies[:7]:
        copy.wait_recv()
    line_ref[y] = summed(row_ref)
    for o in range(1, 4):
        spread(6 + o, line_ref.at[y], line_ref.at[y], in_line(o))
    edges(1)
    for copy in copies[7:10]:
        copy.wait_recv()
    column_ref[core, z] = summed(line_ref)
    for o in range(1, 8):
        spread(32 + o, column_ref.at[core, z], column_ref.at[core, z], in_column(o))
    for copy in copies[10:]:
        copy.wait_recv()
    for side in range(2):
        sum_ref[side * 32:(side + 1) * 32, :] = summed(column_ref, side)

    send_raw(1)
    rotation, restarted = small_step(sum_ref[...] * (1.0 / CELLS), rayleigh_ref[...], order_ref[...], kept_ref[...])
    restarted_ref[...] = restarted
    rotate = rotation_blocks(rotation)

    def speed_row(ref, t):
        return halves([ref[0, pl.ds(t, 1), :], ref[1, pl.ds(t, 1), :]])

    def ax_copy(side):
        return remote(ax_buf.at[side], ax_ref.at[1 - side, RAW:], 17 + side, ax_to[side])

    if RAW < CT:
        for side in range(2):
            a = side * (CA - 1)
            for t in range(RAW, CT):
                value = rotated(rotate, cells_ref[a, :, t * CR:(t + 1) * CR])
                ax_buf[side, t - RAW, 0:KEEP] = value[:KEEP]
                ax_buf[side, t - RAW, KEEP:] = value[KEEP:] * speed_row(speed_ref.at[a], t)

            @pl.when(exists[side])
            def _():
                ax_copy(side).start()

    for side in range(2):
        @pl.loop(0, CA)
        def _(a):
            ang_buf[side, a] = rotated(rotate, edge_ref[side, a])
        copy = remote(ang_buf.at[side], ang_ref.at[1 - side], 15 + side, ang_to[side])
        copy.start()
        copies.append(copy)
    ang_copies = copies[-2:]

    @pl.loop(0, CA)
    def _(a):
        for t in range(CT):
            value = rotated(rotate, cells_ref[a, :, t * CR:(t + 1) * CR])
            for j in range(2):
                part = value[:, j * 128:(j + 1) * 128]
                new_ref[a, t, j] = part
                field_ref[a, t, j, 0:KEEP] = part[:KEEP]
                field_ref[a, t, j, KEEP:] = part[KEEP:] * speed_ref[a, j, t:t + 1, :]

    @pl.loop(0, CA)
    def _(a):
        lanes = iota((64, 128), 1)
        below, above = jnp.maximum(a - 1, 0), jnp.minimum(a + 1, CA - 1)
        has_below, has_above = (a > 0).astype(F32), (a < CA - 1).astype(F32)
        for t in range(CT):
            mid = [field_ref[a, t, j] for j in range(2)]
            up = [pltpu.roll(m, 1, 1) for m in mid]
            down = [pltpu.roll(m, 127, 1) for m in mid]
            behind = [jnp.where(lanes == 0, 0.0, up[0]), jnp.where(lanes == 0, up[0], up[1])]
            ahead = [jnp.where(lanes == 127, down[1], down[0]), jnp.where(lanes == 127, 0.0, down[1])]
            for j in range(2):
                total = field_ref[below, t, j] * has_below + field_ref[above, t, j] * has_above + behind[j] + ahead[j]
                if t > 0:
                    total = total + field_ref[a, t - 1, j]
                if t < CT - 1:
                    total = total + field_ref[a, t + 1, j]
                applied = 6.0 * mid[j] - total
                image_ref[a, t, j, 0:KEEP] = applied[:KEEP] * speed_ref[a, j, t:t + 1, :] - mid[j][:KEEP]
                image_ref[a, t, j, KEEP:] = applied[KEEP:] - new_ref[a, t, j, KEEP:]

    for side in range(2):
        @pl.when(exists[side])
        def _():
            for copy in [near_copy(1 - side)] + raw_copies(1 - side):
                copy.wait_recv()

            @pl.loop(0, RAW)
            def _(t):
                block = stacked(halves([raw_ref[side, 2 * t, 0], raw_ref[side, 2 * t, 1]]),
                                halves([raw_ref[side, 2 * t + 1, 0], raw_ref[side, 2 * t + 1, 1]]))
                value = rotated(rotate, block)
                ax_ref[side, t, 0:KEEP] = value[:KEEP]
                ax_ref[side, t, KEEP:] = value[KEEP:] * speed_row(near_ref.at[side], t)

    for side in range(2):
        ang_copies[1 - side].wait_recv()

        @pl.when(exists[side])
        def _():
            if RAW < CT:
                ax_copy(1 - side).wait_recv()
                ax_copy(side).wait_send()
            for copy in [near_copy(side)] + raw_copies(side):
                copy.wait_send()
    for copy in copies:
        copy.wait_send()


def core_step(right, left, speed, rim, rayleigh, order, kept):
    vmem = pl.BlockSpec(memory_space=pltpu.VMEM)
    main = pl.BlockSpec(memory_space=pltpu.HBM)
    sent = max(CT - RAW, 1)
    inputs = [pltpu.with_memory_space_constraint(v, pltpu.HBM) for v in (right, left, speed, rim, rayleigh, order, kept)]
    return pl.pallas_call(
        core_kernel,
        in_specs=[main] * 7,
        out_specs=[vmem] * 6,
        out_shape=[
            pltpu.VMEM((CA, CT, 2, 64, 128), F32),
            pltpu.VMEM((CA, CT, 2, 64, 128), F32),
            pltpu.VMEM((CA, 2, CT, 128), F32),
            pltpu.VMEM((KEEP, KEEP), F32),
            pltpu.VMEM((2, CA, 64, CR), F32),
            pltpu.VMEM((2, CT, 64, CR), F32),
        ],
        scratch_shapes=[
            pltpu.VMEM((CA, 2 * CT, 2, 64, 128), F32),
            pltpu.VMEM((CA, 256, CT * CR), BF16),
            pltpu.VMEM((CA, CT, 2, 64, 128), F32),
            pltpu.VMEM((128, 256), F32),
            pltpu.VMEM((2, CA, 256, CR), BF16),
            pltpu.VMEM((64, 128), F32),
            pltpu.VMEM((8, 32, 128), F32),
            pltpu.VMEM((4, 32, 128), F32),
            pltpu.VMEM((2, 4, 32, 128), F32),
            pltpu.VMEM((64, 128), F32),
            pltpu.VMEM((2, CA, 64, CR), F32),
            pltpu.VMEM((2, sent, 64, CR), F32),
            pltpu.VMEM((2, 2 * RAW, 2, 64, 128), F32),
            pltpu.VMEM((2, 2, CT, 128), F32),
            pltpu.VMEM((1, CR), jnp.int32),
            pltpu.VMEM((K, K), F32),
            pltpu.VMEM((1, K), jnp.int32),
            pltpu.VMEM((1, KEEP), jnp.int32),
            pltpu.SemaphoreType.DMA((CA,)),
            pltpu.SemaphoreType.DMA((5,)),
            pltpu.SemaphoreType.DMA((41,)),
            pltpu.SemaphoreType.DMA((41,)),
        ],
        compiler_params=pltpu.CompilerParams(collective_id=0, has_side_effects=True, vmem_limit_bytes=44 << 20),
        name="core",
    )(*inputs)


def finish_kernel(new_ref, image_ref, speed_ref, restarted_in, ang_ref, ax_ref, new_right_ref, new_left_ref,
                  right_image_ref, left_image_ref, restarted_ref, fix_ref, sem):
    slab = lax.axis_index("slab")
    outs = (new_right_ref, new_left_ref, right_image_ref, left_image_ref)

    def send(n, src, a, t):
        for j in range(2):
            low = (n % 2) * KEEP
            pltpu.make_async_copy(src.at[t, j, low:low + KEEP], outs[n].at[:, a, j, t, :], sem.at[n]).start()

    @pl.loop(0, CA)
    def _(a):
        for t in range(CT):
            send(0, new_ref.at[a], a, t)
            send(1, new_ref.at[a], a, t)

    @pl.loop(1, CA - 1)
    def _(a):
        for t in range(1, CT - 1):
            send(2, image_ref.at[a], a, t)
            send(3, image_ref.at[a], a, t)

    @pl.loop(0, CA)
    def _(a):
        def fix(t):
            for j in range(2):
                lanes = slice(j * 128, (j + 1) * 128)
                halo = jnp.zeros((64, 128), F32)
                if t == 0:
                    halo = halo + ang_ref[0, a, :, lanes]
                if t == CT - 1:
                    halo = halo + ang_ref[1, a, :, lanes]
                halo = halo + jnp.where(jnp.logical_and(a == 0, slab > 0), ax_ref[0, t, :, lanes], 0.0)
                halo = halo + jnp.where(jnp.logical_and(a == CA - 1, slab < 7), ax_ref[1, t, :, lanes], 0.0)
                value = image_ref[a, t, j]
                fix_ref[a, t, j, 0:KEEP] = value[:KEEP] - halo[:KEEP] * speed_ref[a, j, t:t + 1, :]
                fix_ref[a, t, j, KEEP:] = value[KEEP:] - halo[KEEP:]
            send(2, fix_ref.at[a], a, t)
            send(3, fix_ref.at[a], a, t)

        for t in (0, CT - 1):
            fix(t)

        @pl.when(jnp.logical_or(a == 0, a == CA - 1))
        def _():
            for t in range(1, CT - 1):
                fix(t)

    restarted_ref[...] = restarted_in[...]
    for n in range(4):
        pltpu.make_async_copy(outs[n], outs[n], sem.at[n]).wait()


def finish(*arrays):
    vmem = pl.BlockSpec(memory_space=pltpu.VMEM)
    main = pl.BlockSpec(memory_space=pltpu.HBM)
    kept = jax.ShapeDtypeStruct((KEEP, CA, 2, CT, 128), F32)
    return pl.pallas_call(
        finish_kernel,
        in_specs=[vmem] * 6,
        out_specs=[main] * 4 + [vmem],
        out_shape=[kept] * 4 + [jax.ShapeDtypeStruct((KEEP, KEEP), F32)],
        scratch_shapes=[pltpu.VMEM((CA, CT, 2, 64, 128), F32), pltpu.SemaphoreType.DMA((4,))],
        compiler_params=pltpu.CompilerParams(vmem_limit_bytes=10 << 20),
        name="finish",
    )(*[pltpu.with_memory_space_constraint(v, pltpu.VMEM) for v in arrays])


def tiles(array):
    return array.reshape(array.shape[0], CT, CA, 2, 128).transpose(0, 2, 3, 1, 4)


def local(right_basis, left_basis, speed_squared, rayleigh, schur_order, kept_index, rim_map):
    right, left, speed = tiles(right_basis), tiles(left_basis), tiles(speed_squared[None])[0]
    *outs, restarted = finish(*core_step(
        right, left, speed, rim_map.reshape(1, CR), rayleigh, schur_order.reshape(1, K), kept_index.reshape(1, KEEP)))
    shape = (KEEP, CT, CA, CR)
    return tuple(o.transpose(0, 3, 1, 2, 4).reshape(shape) for o in outs) + (restarted,)


def solution(mesh):
    fields = P(None, "sector", "slab", None)
    return jax.shard_map(
        local,
        mesh=mesh,
        in_specs=(fields, fields, P("sector", "slab", None), P(), P(), P(), P()),
        out_specs=(fields, fields, fields, fields, P()),
        check_vma=False,
    )
```

```python
import jax
import jax.numpy as jnp
from jax import lax
from jax.experimental import pallas as pl
from jax.experimental.pallas import tpu as pltpu
from jax.sharding import PartitionSpec as P

MESH = pl.DeviceIdType.MESH
NN = (((1,), (0,)), ((), ()))
NT = (((1,), (1,)), ((), ()))
TN = (((0,), (0,)), ((), ()))
F32 = jnp.float32
BF16 = jnp.bfloat16
K, KEEP, CT, CA, CR = 64, 32, 8, 12, 256
CELLS = 3145728
SENT = (6, 8)
RAW = SENT[-1] // 2
AHEAD = 4


def mm(a, b, dims=NN):
    return lax.dot_general(a, b, dims, precision=lax.Precision.HIGHEST, preferred_element_type=F32)


def mm16(a, b, dims=NN):
    return lax.dot_general(a, b, dims, preferred_element_type=F32)


def iota(shape, dim):
    return lax.broadcasted_iota(jnp.int32, shape, dim)


def split(x):
    high = x.astype(BF16)
    return high, (x - high.astype(F32)).astype(BF16)


def stacked(right, left):
    return jnp.concatenate(split(right) + split(left), axis=0)


def halves(pair):
    return jnp.concatenate(pair, axis=1)


def place(sector, slab):
    return sector // 4, slab // 2, (slab % 2) * 2 + (sector // 2) % 2, sector % 2


def device(x, y, z, core):
    return (x * 4 + (z % 2) * 2 + core, y * 2 + z // 2)


def combined(part):
    top = part[:64] + part[64:]
    gram, cross = top[:, :128], top[:, 128:]
    gram, cross = gram + pltpu.roll(gram, 64, 1), cross + pltpu.roll(cross, 64, 1)
    return jnp.where(iota((64, 128), 1) < 64, gram, cross)


def pivots(group, first):
    rows = iota((8, 128), 0)
    top = first // 8
    states = []
    for blocks in group:
        columns = [[jnp.broadcast_to(blocks[i][:, first + j:first + j + 1], (8, 128)) for i in range(top, 8)] for j in range(8)]
        corner = [[columns[j][0][i:i + 1, :] for j in range(8)] for i in range(8)]
        states.append((columns, corner, [blocks[top][i:i + 1, :] for i in range(8)], []))
    for j in range(8):
        for columns, corner, lead, scaled in states:
            inverse = 1.0 / corner[j][j]
            scaled.append(lead[j] * inverse)
            for m in range(j + 1, 8):
                factor = corner[m][j] * inverse
                for i in range(m, 8):
                    corner[i][m] = corner[i][m] - corner[i][j] * factor
                lead[m] = lead[m] - corner[m][j] * scaled[j]
                columns[m] = [c - d * factor for c, d in zip(columns[m], columns[j])]
    result = []
    for blocks, (columns, _, _, scaled) in zip(group, states):
        blocks = list(blocks)
        for i in range(top, 8):
            for j in range(8):
                column = columns[j][i - top]
                if i == top:
                    column = jnp.where(rows > j, column, 0.0)
                blocks[i] = blocks[i] - column * scaled[j]
        result.append(blocks)
    return result


def eliminate(arrays):
    rows, lanes = iota((8, 128), 0), iota((8, 128), 1)
    group = [[a[8 * i:8 * i + 8, :] for i in range(8)] for a in arrays]
    for first in range(0, 64, 8):
        group = pivots(group, first)
    result = []
    for blocks in group:
        scaled = []
        for i, block in enumerate(blocks):
            pivot = jnp.sum(jnp.where(lanes == rows + 8 * i, block, 0.0), axis=1, keepdims=True)
            scaled.append(block * lax.rsqrt(pivot))
        full = jnp.concatenate(scaled, axis=0)
        keep = jnp.logical_or(iota((64, 128), 1) >= 64, iota((64, 128), 1) >= iota((64, 128), 0))
        result.append(jnp.where(keep, full, 0.0))
    return result


def small_step(gc, rayleigh, order, kept):
    r64, c64 = iota((64, 64), 0), iota((64, 64), 1)
    eye = (r64 == c64).astype(F32)
    order_col = jnp.sum(jnp.where(r64 == c64, order, 0).astype(F32), axis=1, keepdims=True).astype(jnp.int32)
    kept_col = jnp.sum(jnp.where(iota((32, 32), 0) == iota((32, 32), 1), kept, 0).astype(F32), axis=1, keepdims=True).astype(jnp.int32)
    select_order = (order_col == c64).astype(F32)
    select_kept = (kept_col == iota((32, 64), 1)).astype(F32)
    cross_t = gc[:, 64:]
    a1 = jnp.concatenate([gc[:, :64], eye], axis=1)
    a2 = jnp.concatenate([mm(cross_t, cross_t, NT), eye], axis=1)
    a1, a2 = eliminate([a1, a2])
    lower_t, lower_inv, cross_low = a1[:, :64], a1[:, 64:], a2[:, 64:]
    side = mm(lower_inv, rayleigh, NT)
    ordered = mm(select_order, jnp.concatenate([lower_t, side], axis=1))
    permuted_t = mm(ordered[:, 64:], ordered[:, :64], NT)
    a3 = jnp.concatenate([mm(permuted_t, permuted_t, NT), permuted_t], axis=1)
    cross_inv = mm(cross_low, mm(cross_low, cross_t), TN)
    cross_inv = cross_inv + mm(cross_inv, eye - mm(cross_t, cross_inv, TN))
    tail = jnp.concatenate([lower_inv, mm(lower_t, cross_inv)], axis=1)
    basis_t = eliminate([a3])[0][:, 64:]
    weight = jnp.where(r64 > c64, 1.0, jnp.where(r64 == c64, 0.5, 0.0))
    basis_t = basis_t - mm((mm(basis_t, basis_t, NT) - eye) * weight, basis_t)
    change = (mm(basis_t, basis_t, NT) - eye) * weight
    chosen = select_kept - mm(select_kept, change)
    kept_t = mm(chosen, basis_t)
    restarted = mm(mm(kept_t, permuted_t, NT), kept_t, NT)
    return mm(chosen, mm(basis_t, tail)), restarted


def rotation_blocks(rotation):
    high, low = split(rotation)
    zero = jnp.zeros((KEEP, 128), BF16)

    def both(part):
        right, left = part[:, :64], part[:, 64:]
        return [
            jnp.concatenate([right, right, zero], axis=1),
            jnp.concatenate([zero, left, left], axis=1),
        ]

    return jnp.concatenate(both(high) + both(low), axis=0)


def rotated(rotate, block):
    both = mm16(rotate, block)
    return both[:64] + both[64:]


def core_kernel(right_ref, left_ref, speed_hbm, rim_hbm, rayleigh_hbm, order_hbm, kept_hbm,
                new_ref, image_ref, speed_ref, restarted_ref, ang_ref, ax_ref,
                buf_ref, cells_ref, field_ref, acc_ref, edge_ref, part_ref, row_ref, line_ref, column_ref, sum_ref, ang_buf, ax_buf, raw_ref,
                near_ref, rim_ref, rayleigh_ref, order_ref, kept_ref, load_sem, small_sem, send_sem, recv_sem):
    small = [pltpu.make_async_copy(src, dst, small_sem.at[i]) for i, (src, dst) in enumerate((
        (speed_hbm, speed_ref), (rim_hbm, rim_ref), (rayleigh_hbm, rayleigh_ref), (order_hbm, order_ref), (kept_hbm, kept_ref)))]
    for copy in small:
        copy.start()
    refs = (right_ref, left_ref)
    sector, slab = lax.axis_index("sector"), lax.axis_index("slab")
    x, y, z, core = place(sector, slab)
    lane, column = 2 * x + core, 2 * z + core

    def in_row(o):
        other = lax.rem(lane + o, 8)
        return lax.rem(other, 2), device(other // 2, y, z, lax.rem(other, 2))

    def in_line(o):
        return device(x, lax.rem(y + o, 4), z, core)

    def in_column(o):
        other = lax.rem(column + o, 8)
        return device(x, y, other // 2, lax.rem(other, 2))

    ang_to = ((lax.rem(sector + 15, 16), slab), (lax.rem(sector + 1, 16), slab))
    ax_to = ((sector, lax.rem(slab + 7, 8)), (sector, lax.rem(slab + 1, 8)))
    exists = (slab > 0, slab < 7)

    barrier = pltpu.get_barrier_semaphore()
    for peer in ([in_row(o)[1] for o in range(1, 8)] + [in_line(o) for o in range(1, 4)]
                 + [in_column(o) for o in range(1, 8)] + list(ang_to + ax_to)):
        pl.semaphore_signal(barrier, inc=1, device_id=peer, device_id_type=MESH)

    def load(i):
        a = lax.rem(CA - i, CA)
        for n in range(2):
            for t in range(CT):
                for j in range(2):
                    pltpu.make_async_copy(refs[n].at[:, a, j, t, :], buf_ref.at[a, 2 * t + n, j], load_sem.at[a]).start()

    @pl.loop(0, AHEAD)
    def _(i):
        load(i)

    def remote(src, dst, n, peer):
        return pltpu.make_async_remote_copy(
            src_ref=src, dst_ref=dst, send_sem=send_sem.at[n], recv_sem=recv_sem.at[n],
            device_id=peer, device_id_type=MESH)

    def near_copy(side):
        return remote(speed_ref.at[side * (CA - 1)], near_ref.at[1 - side], 11 + side, ax_to[side])

    def raw_copies(side, stage=None):
        a = side * (CA - 1)
        copies = []
        for i in range(len(SENT)):
            units = slice(SENT[i - 1] if i else 0, SENT[i])
            if units.start < units.stop and stage in (None, i):
                copies.append(remote(buf_ref.at[a, units], raw_ref.at[1 - side, units], 19 + 2 * i + side, ax_to[side]))
        return copies

    def send_raw(stage):
        if stage and SENT[stage] == SENT[stage - 1]:
            return
        for side in range(2):
            @pl.when(exists[side])
            def _():
                for copy in raw_copies(side, stage):
                    copy.start()

    for copy in small:
        copy.wait()
    acc_ref[...] = jnp.zeros_like(acc_ref)
    hot = (iota((CR, CR), 0) == rim_ref[...]).astype(BF16)

    @pl.loop(0, CA)
    def _(i):
        a = lax.rem(CA - i, CA)

        @pl.when(i + AHEAD < CA)
        def _():
            load(i + AHEAD)

        pltpu.make_async_copy(buf_ref.at[a], buf_ref.at[a], load_sem.at[a]).wait()
        for side in range(2):
            @pl.when(i == side)
            def _():
                if side == 0:
                    pl.semaphore_wait(barrier, 21)
                if True:
                    @pl.when(exists[side])
                    def _():
                        for copy in [near_copy(side)] + raw_copies(side, 0):
                            copy.start()

        columns = []
        for t in range(CT):
            for j in range(2):
                columns.append(stacked(buf_ref[a, 2 * t, j], buf_ref[a, 2 * t + 1, j]))
        block = halves(columns)
        cells_ref[a] = block
        acc_ref[...] += mm16(block[:128], block, NT)

    part_ref[...] = combined(acc_ref[...])

    def edges(side):
        t = side * (CT - 1)

        @pl.loop(0, CA)
        def _(a):
            scaled = halves([speed_ref[a, j, t:t + 1, :] * buf_ref[a, 2 * t + 1, j] for j in range(2)])
            edge = jnp.concatenate((cells_ref[a, 0:128, t * CR:(t + 1) * CR],) + split(scaled), axis=0)
            edge_ref[side, a] = mm16(edge, hot, NT if side else NN).astype(BF16)

    def half(h):
        return pl.ds(pl.multiple_of(h * 32, 32), 32)

    def summed(ref, *lead):
        parts = [ref[lead + (i,)] for i in range(ref.shape[len(lead)])]
        while len(parts) > 1:
            parts = [parts[i] + parts[i + 1] for i in range(0, len(parts), 2)]
        return parts[0]

    copies = []

    def spread(n, src, dst, peer):
        copy = remote(src, dst, n, peer)
        copy.start()
        copies.append(copy)

    for o in range(1, 8):
        side, peer = in_row(o)
        spread(o - 1, part_ref.at[half(side)], row_ref.at[lane], peer)
    row_ref[lane] = part_ref[half(core), :]
    edges(0)
    for copy in copies[:7]:
        copy.wait_recv()
    line_ref[y] = summed(row_ref)
    for o in range(1, 4):
        spread(6 + o, line_ref.at[y], line_ref.at[y], in_line(o))
    edges(1)
    for copy in copies[7:10]:
        copy.wait_recv()
    column_ref[core, z] = summed(line_ref)
    for o in range(1, 8):
        spread(32 + o, column_ref.at[core, z], column_ref.at[core, z], in_column(o))
    for copy in copies[10:]:
        copy.wait_recv()
    for side in range(2):
        sum_ref[side * 32:(side + 1) * 32, :] = summed(column_ref, side)

    send_raw(1)
    rotation, restarted = small_step(sum_ref[...] * (1.0 / CELLS), rayleigh_ref[...], order_ref[...], kept_ref[...])
    restarted_ref[...] = restarted
    rotate = rotation_blocks(rotation)

    def speed_row(ref, t):
        return halves([ref[0, pl.ds(t, 1), :], ref[1, pl.ds(t, 1), :]])

    def ax_copy(side):
        return remote(ax_buf.at[side], ax_ref.at[1 - side, RAW:], 17 + side, ax_to[side])

    if RAW < CT:
        for side in range(2):
            a = side * (CA - 1)
            for t in range(RAW, CT):
                value = rotated(rotate, cells_ref[a, :, t * CR:(t + 1) * CR])
                ax_buf[side, t - RAW, 0:KEEP] = value[:KEEP]
                ax_buf[side, t - RAW, KEEP:] = value[KEEP:] * speed_row(speed_ref.at[a], t)

            @pl.when(exists[side])
            def _():
                ax_copy(side).start()

    for side in range(2):
        @pl.loop(0, CA)
        def _(a):
            ang_buf[side, a] = rotated(rotate, edge_ref[side, a])
        copy = remote(ang_buf.at[side], ang_ref.at[1 - side], 15 + side, ang_to[side])
        copy.start()
        copies.append(copy)
    ang_copies = copies[-2:]

    @pl.loop(0, CA)
    def _(a):
        for t in range(CT):
            value = rotated(rotate, cells_ref[a, :, t * CR:(t + 1) * CR])
            for j in range(2):
                part = value[:, j * 128:(j + 1) * 128]
                new_ref[a, t, j] = part
                field_ref[a, t, j, 0:KEEP] = part[:KEEP]
                field_ref[a, t, j, KEEP:] = part[KEEP:] * speed_ref[a, j, t:t + 1, :]

    @pl.loop(0, CA)
    def _(a):
        lanes = iota((64, 128), 1)
        below, above = jnp.maximum(a - 1, 0), jnp.minimum(a + 1, CA - 1)
        has_below, has_above = (a > 0).astype(F32), (a < CA - 1).astype(F32)
        for t in range(CT):
            mid = [field_ref[a, t, j] for j in range(2)]
            up = [pltpu.roll(m, 1, 1) for m in mid]
            down = [pltpu.roll(m, 127, 1) for m in mid]
            behind = [jnp.where(lanes == 0, 0.0, up[0]), jnp.where(lanes == 0, up[0], up[1])]
            ahead = [jnp.where(lanes == 127, down[1], down[0]), jnp.where(lanes == 127, 0.0, down[1])]
            for j in range(2):
                total = field_ref[below, t, j] * has_below + field_ref[above, t, j] * has_above + behind[j] + ahead[j]
                if t > 0:
                    total = total + field_ref[a, t - 1, j]
                if t < CT - 1:
                    total = total + field_ref[a, t + 1, j]
                applied = 6.0 * mid[j] - total
                image_ref[a, t, j, 0:KEEP] = applied[:KEEP] * speed_ref[a, j, t:t + 1, :] - mid[j][:KEEP]
                image_ref[a, t, j, KEEP:] = applied[KEEP:] - new_ref[a, t, j, KEEP:]

    for side in range(2):
        @pl.when(exists[side])
        def _():
            for copy in [near_copy(1 - side)] + raw_copies(1 - side):
                copy.wait_recv()

            @pl.loop(0, RAW)
            def _(t):
                block = stacked(halves([raw_ref[side, 2 * t, 0], raw_ref[side, 2 * t, 1]]),
                                halves([raw_ref[side, 2 * t + 1, 0], raw_ref[side, 2 * t + 1, 1]]))
                value = rotated(rotate, block)
                ax_ref[side, t, 0:KEEP] = value[:KEEP]
                ax_ref[side, t, KEEP:] = value[KEEP:] * speed_row(near_ref.at[side], t)

    for side in range(2):
        ang_copies[1 - side].wait_recv()

        @pl.when(exists[side])
        def _():
            if RAW < CT:
                ax_copy(1 - side).wait_recv()
                ax_copy(side).wait_send()
            for copy in [near_copy(side)] + raw_copies(side):
                copy.wait_send()
    for copy in copies:
        copy.wait_send()


def core_step(right, left, speed, rim, rayleigh, order, kept):
    vmem = pl.BlockSpec(memory_space=pltpu.VMEM)
    main = pl.BlockSpec(memory_space=pltpu.HBM)
    sent = max(CT - RAW, 1)
    inputs = [pltpu.with_memory_space_constraint(v, pltpu.HBM) for v in (right, left, speed, rim, rayleigh, order, kept)]
    return pl.pallas_call(
        core_kernel,
        in_specs=[main] * 7,
        out_specs=[vmem] * 6,
        out_shape=[
            pltpu.VMEM((CA, CT, 2, 64, 128), F32),
            pltpu.VMEM((CA, CT, 2, 64, 128), F32),
            pltpu.VMEM((CA, 2, CT, 128), F32),
            pltpu.VMEM((KEEP, KEEP), F32),
            pltpu.VMEM((2, CA, 64, CR), F32),
            pltpu.VMEM((2, CT, 64, CR), F32),
        ],
        scratch_shapes=[
            pltpu.VMEM((CA, 2 * CT, 2, 64, 128), F32),
            pltpu.VMEM((CA, 256, CT * CR), BF16),
            pltpu.VMEM((CA, CT, 2, 64, 128), F32),
            pltpu.VMEM((128, 256), F32),
            pltpu.VMEM((2, CA, 256, CR), BF16),
            pltpu.VMEM((64, 128), F32),
            pltpu.VMEM((8, 32, 128), F32),
            pltpu.VMEM((4, 32, 128), F32),
            pltpu.VMEM((2, 4, 32, 128), F32),
            pltpu.VMEM((64, 128), F32),
            pltpu.VMEM((2, CA, 64, CR), F32),
            pltpu.VMEM((2, sent, 64, CR), F32),
            pltpu.VMEM((2, 2 * RAW, 2, 64, 128), F32),
            pltpu.VMEM((2, 2, CT, 128), F32),
            pltpu.VMEM((1, CR), jnp.int32),
            pltpu.VMEM((K, K), F32),
            pltpu.VMEM((1, K), jnp.int32),
            pltpu.VMEM((1, KEEP), jnp.int32),
            pltpu.SemaphoreType.DMA((CA,)),
            pltpu.SemaphoreType.DMA((5,)),
            pltpu.SemaphoreType.DMA((41,)),
            pltpu.SemaphoreType.DMA((41,)),
        ],
        compiler_params=pltpu.CompilerParams(collective_id=0, has_side_effects=True, vmem_limit_bytes=44 << 20),
        name="core",
    )(*inputs)


def finish_kernel(new_ref, image_ref, speed_ref, restarted_in, ang_ref, ax_ref, new_right_ref, new_left_ref,
                  right_image_ref, left_image_ref, restarted_ref, fix_ref, sem):
    slab = lax.axis_index("slab")
    outs = (new_right_ref, new_left_ref, right_image_ref, left_image_ref)

    def send(n, src, a, t):
        for j in range(2):
            low = (n % 2) * KEEP
            pltpu.make_async_copy(src.at[t, j, low:low + KEEP], outs[n].at[:, a, j, t, :], sem.at[n]).start()

    @pl.loop(0, CA)
    def _(a):
        for t in range(CT):
            send(0, new_ref.at[a], a, t)
            send(1, new_ref.at[a], a, t)

    @pl.loop(1, CA - 1)
    def _(a):
        for t in range(1, CT - 1):
            send(2, image_ref.at[a], a, t)
            send(3, image_ref.at[a], a, t)

    @pl.loop(0, CA)
    def _(a):
        def fix(t):
            for j in range(2):
                lanes = slice(j * 128, (j + 1) * 128)
                halo = jnp.zeros((64, 128), F32)
                if t == 0:
                    halo = halo + ang_ref[0, a, :, lanes]
                if t == CT - 1:
                    halo = halo + ang_ref[1, a, :, lanes]
                halo = halo + jnp.where(jnp.logical_and(a == 0, slab > 0), ax_ref[0, t, :, lanes], 0.0)
                halo = halo + jnp.where(jnp.logical_and(a == CA - 1, slab < 7), ax_ref[1, t, :, lanes], 0.0)
                value = image_ref[a, t, j]
                fix_ref[a, t, j, 0:KEEP] = value[:KEEP] - halo[:KEEP] * speed_ref[a, j, t:t + 1, :]
                fix_ref[a, t, j, KEEP:] = value[KEEP:] - halo[KEEP:]
            send(2, fix_ref.at[a], a, t)
            send(3, fix_ref.at[a], a, t)

        for t in (0, CT - 1):
            fix(t)

        @pl.when(jnp.logical_or(a == 0, a == CA - 1))
        def _():
            for t in range(1, CT - 1):
                fix(t)

    restarted_ref[...] = restarted_in[...]
    for n in range(4):
        pltpu.make_async_copy(outs[n], outs[n], sem.at[n]).wait()


def finish(*arrays):
    vmem = pl.BlockSpec(memory_space=pltpu.VMEM)
    main = pl.BlockSpec(memory_space=pltpu.HBM)
    kept = jax.ShapeDtypeStruct((KEEP, CA, 2, CT, 128), F32)
    return pl.pallas_call(
        finish_kernel,
        in_specs=[vmem] * 6,
        out_specs=[main] * 4 + [vmem],
        out_shape=[kept] * 4 + [jax.ShapeDtypeStruct((KEEP, KEEP), F32)],
        scratch_shapes=[pltpu.VMEM((CA, CT, 2, 64, 128), F32), pltpu.SemaphoreType.DMA((4,))],
        compiler_params=pltpu.CompilerParams(vmem_limit_bytes=10 << 20),
        name="finish",
    )(*[pltpu.with_memory_space_constraint(v, pltpu.VMEM) for v in arrays])


def tiles(array):
    return array.reshape(array.shape[0], CT, CA, 2, 128).transpose(0, 2, 3, 1, 4)


def local(right_basis, left_basis, speed_squared, rayleigh, schur_order, kept_index, rim_map):
    right, left, speed = tiles(right_basis), tiles(left_basis), tiles(speed_squared[None])[0]
    *outs, restarted = finish(*core_step(
        right, left, speed, rim_map.reshape(1, CR), rayleigh, schur_order.reshape(1, K), kept_index.reshape(1, KEEP)))
    shape = (KEEP, CT, CA, CR)
    return tuple(o.transpose(0, 3, 1, 2, 4).reshape(shape) for o in outs) + (restarted,)


def solution(mesh):
    fields = P(None, "sector", "slab", None)
    return jax.shard_map(
        local,
        mesh=mesh,
        in_specs=(fields, fields, P("sector", "slab", None), P(), P(), P(), P()),
        out_specs=(fields, fields, fields, fields, P()),
        check_vma=False,
    )
```
